32 devices in a mesh: nodes: 8 (over y, x, core), cols: 4 (over z).
Axes of the slice: x: 2, y: 2, z: 4, core: 2. Of those that a mesh axis runs over, the one named last changes fastest.
Arguments:
- features: bfloat16 [1024, 512], P('nodes', 'cols'), may hold values from -6 to 6
- weight: bfloat16 [512, 512], P(None, 'cols'), may hold values from -0.25 to 0.25
- degree: int32 [1024], P('nodes'), may hold values from 1 to 64
- tile_cols: int32 [8, 8], P('nodes'), may hold values from 0 to 7, as said below
- tile_count: int32 [8], P('nodes'), may hold values from 1 to 8, as said below
- tile_codes: int32 [8, 8], P('nodes'), may hold values from 0 to 1048575
- cotangent: bfloat16 [1024, 512], P('nodes', 'cols'), may hold values from -6 to 6
Outputs:
- activation: bfloat16 [1024, 512], P('nodes', 'cols')
- weight_grad: float32 [512, 512], P(None, 'cols')
- feats_grad: float32 [1024, 512], P('nodes', 'cols')
The draws below stay inside these ranges and needn't reach their ends.
Inputs may be any that keep to these rules, and one draw needn't show every extreme that they name: `tile_cols`: each row lists every node block once, and row i begins with block i. The tiles of row block i are those of its first tile_count[i] slots; some row block holds all 8.
All inputs are finite; a program needn't handle non-finite values.
Results may differ from the reference program's by a relative error of at most 0.0065.
Values may be sent and summed in bfloat16 or wider, within the bound.
A program may use at most 64 MiB of HBM per device.

```python
import jax
import jax.numpy as jnp
from jax import lax

H = 512
TILE = 128
BLOCKS = 8
NODES = 1024


def draw_tile_cols(key, part):
    keys = jax.random.split(key, BLOCKS)
    shuffled = jax.vmap(lambda one_key: jax.random.permutation(one_key, BLOCKS - 1))(keys).astype(jnp.int32)
    offsets = jnp.concatenate([jnp.zeros((BLOCKS, 1), jnp.int32), shuffled + 1], axis=1)
    row_ids = jnp.arange(BLOCKS, dtype=jnp.int32)[:, None]
    return ((row_ids + offsets) % BLOCKS).astype(jnp.int32)


def draw_tile_count(key, part):
    first_key, second_key = jax.random.split(key)
    drawn = jax.random.randint(first_key, (BLOCKS,), 1, BLOCKS + 1, dtype=jnp.int32)
    counts = jnp.maximum(drawn * (drawn + BLOCKS) // (2 * BLOCKS), 1)
    fullest = jax.random.randint(second_key, (), 0, BLOCKS, dtype=jnp.int32)
    return jnp.where(jnp.arange(BLOCKS, dtype=jnp.int32) == fullest, BLOCKS, counts).astype(jnp.int32)


def set_ends(values, own_key, least, high):
    shape = values.shape
    place = [jax.random.randint(jax.random.fold_in(own_key, axis), (), 0, shape[axis]) for axis in range(len(shape))]
    values = values.at[tuple(place)].set(least)
    longest = shape.index(max(shape))
    place[longest] = (place[longest] + 1) % shape[longest]
    return values.at[tuple(place)].set(high)


def steps_of(key, dims, shards, smallest, high):
    loudness, own = 1.0, jax.random.fold_in(key, 6)
    for axis_at, blocks in shards:
        heights = jnp.exp(jax.random.uniform(jax.random.fold_in(own, axis_at), (blocks,), jnp.float32, smallest / len(shards), high / len(shards)))
        loudness = loudness * jnp.repeat(heights, dims[axis_at] // blocks).reshape([-1 if axis == axis_at else 1 for axis in range(len(dims))])
    return loudness


def centred(own_key, dims, deviation, most, cuts=(), kind=jnp.bfloat16):
    values = jax.random.normal(own_key, dims, jnp.float32) * deviation
    if len(cuts) > 0:
        values = steps_of(own_key, dims, cuts, -0.22, 0.18) * values
    return jnp.clip(values, min=-most, max=most).astype(kind)


def setup_inputs(seed: int = 0) -> dict:
    splits = jax.random.split(jax.random.key(seed), 8)
    return {
        "features": centred(splits[0], (NODES, H), 1.0, 6.0, ((0, 8), (1, 4))),
        "weight": centred(splits[1], (H, H), H ** -0.5, 0.25, ((1, 4),)),
        "degree": set_ends(jax.random.randint(splits[2], (NODES,), 1, 65), jax.random.fold_in(splits[2], 1), 1, 64).astype(jnp.int32),
        "tile_cols": draw_tile_cols(jax.random.fold_in(splits[7], 71), 0),
        "tile_count": draw_tile_count(jax.random.fold_in(splits[7], 71), 0),
        "tile_codes": set_ends(jax.random.randint(splits[5], (BLOCKS, BLOCKS), 0, 1048576), jax.random.fold_in(splits[5], 1), 0, 1048575).astype(jnp.int32),
        "cotangent": centred(splits[6], (NODES, H), 1.0, 6.0, ((0, 8), (1, 4))),
    }


def tile_bits(pattern_code):
    line_ids = jnp.arange(TILE, dtype=jnp.int32)
    hashed = pattern_code[..., None, None] * 73856093 ^ line_ids[:, None] * 19349663 ^ line_ids[None, :] * 83492791
    hashed = hashed ^ hashed >> 13
    hashed = hashed * 1274126177
    hashed = hashed ^ hashed >> 16
    return hashed & 63 == 0

def make_tiles(matches, code_table, live_limit, own, identity):
    slot_ids = jnp.arange(matches.shape[1], dtype=jnp.int32)
    slot_index = lax.optimization_barrier(jnp.sum(jnp.where(matches, slot_ids[None, :], 0), axis=1, dtype=jnp.int32))
    code_value = lax.optimization_barrier(jnp.sum(jnp.where(matches, code_table, 0), axis=1, dtype=jnp.int32))
    pattern = tile_bits(code_value) & (slot_index < live_limit)[:, None, None]
    values = pattern.astype(jnp.float32) + jnp.where(own, 1.0, 0.0).astype(jnp.float32)[:, None, None] * identity
    return values.astype(jnp.bfloat16)

def reference(features, weight, degree, tile_cols, tile_count, tile_codes, cotangent):
    blocks = tile_cols.shape[0]
    block_ids = jnp.arange(blocks, dtype=jnp.int32)
    identity = jnp.eye(TILE, dtype=jnp.float32)
    inv_root = lax.rsqrt(degree.astype(jnp.float32))[:, None]
    scaled = (features.astype(jnp.float32) * inv_root).astype(jnp.bfloat16)
    scaled_wide = lax.optimization_barrier(scaled).astype(jnp.float32)

    def adjacency_rows(row):
        matches = tile_cols[row][None, :] == block_ids[:, None]
        tiles = make_tiles(matches, tile_codes[row][None, :], tile_count[row], block_ids == row, identity)
        return jnp.transpose(tiles.astype(jnp.float32), (1, 0, 2)).reshape(TILE, blocks * TILE)

    def forward_rows(row):
        return jnp.dot(adjacency_rows(row), scaled_wide, preferred_element_type=jnp.float32)
    gathered = lax.map(forward_rows, block_ids).reshape(blocks * TILE, H)
    aggregated = (inv_root * gathered).astype(jnp.bfloat16)
    pre = jnp.dot(aggregated, weight, preferred_element_type=jnp.float32)
    activation = jax.nn.silu(pre).astype(jnp.bfloat16)
    sigma = jax.nn.sigmoid(pre)
    grad_pre = (cotangent.astype(jnp.float32) * sigma * (1.0 + pre * (1.0 - sigma))).astype(jnp.bfloat16)
    weight_grad = lax.dot_general(aggregated, grad_pre, (((0,), (0,)), ((), ())), preferred_element_type=jnp.float32)
    grad_agg = lax.dot_general(grad_pre, weight, (((1,), (1,)), ((), ())), preferred_element_type=jnp.float32)
    grad_scaled = (inv_root * grad_agg).astype(jnp.bfloat16)
    grad_wide = lax.optimization_barrier(grad_scaled).astype(jnp.float32)

    def backward_rows(total, row):
        block_grad = lax.dynamic_slice_in_dim(grad_wide, row * TILE, TILE, 0)
        term = lax.dot_general(adjacency_rows(row), block_grad, (((0,), (0,)), ((), ())), preferred_element_type=jnp.float32)
        return (total + term, None)
    back_total, _ = lax.scan(backward_rows, jnp.zeros((blocks * TILE, H), jnp.float32), block_ids)
    feats_grad = inv_root * back_total
    return (activation, weight_grad, feats_grad)
```

```python
import functools

import jax
import jax.numpy as jnp
from jax import lax
from jax.experimental import pallas as pl
from jax.experimental.pallas import tpu as pltpu
from jax.sharding import PartitionSpec as P

MESH = pl.DeviceIdType.MESH

TILE = 128


def tile_bits(pattern_code):
    line_ids = jnp.arange(TILE, dtype=jnp.int32)
    hashed = (
        pattern_code[..., None, None] * 73856093
        ^ line_ids[:, None] * 19349663
        ^ line_ids[None, :] * 83492791
    )
    hashed = hashed ^ hashed >> 13
    hashed = hashed * 1274126177
    hashed = hashed ^ hashed >> 16
    return hashed & 63 == 0


def make_tiles(matches, code_table, live_limit, own, identity):
    slot_ids = jnp.arange(matches.shape[1], dtype=jnp.int32)
    slot_index = jnp.sum(jnp.where(matches, slot_ids[None, :], 0), axis=1, dtype=jnp.int32)
    code_value = jnp.sum(jnp.where(matches, code_table, 0), axis=1, dtype=jnp.int32)
    pattern = tile_bits(code_value) & (slot_index < live_limit)[:, None, None]
    values = (
        pattern.astype(jnp.float32)
        + jnp.where(own, 1.0, 0.0).astype(jnp.float32)[:, None, None] * identity
    )
    return values.astype(jnp.bfloat16)


def body(features, weight, degree, tile_cols, tile_count, tile_codes, cotangent):
    my_block = lax.axis_index("nodes")
    identity = jnp.eye(TILE, dtype=jnp.float32)
    inv_root = lax.rsqrt(degree.astype(jnp.float32))[:, None]
    scaled = (features.astype(jnp.float32) * inv_root).astype(jnp.bfloat16)
    my_cols = tile_cols[0]
    my_codes = tile_codes[0]
    my_count = tile_count[0]
    pieces = lax.all_gather(scaled[None], "nodes", axis=0, tiled=True)
    count_blocks = pieces.shape[0]
    targets = jnp.arange(count_blocks, dtype=jnp.int32)
    matches = targets[:, None] == my_cols[None, :]
    tiles = make_tiles(matches, my_codes[None, :], my_count, targets == my_block, identity)
    gathered = lax.dot_general(
        tiles, pieces, (((0, 2), (0, 1)), ((), ())), preferred_element_type=jnp.float32
    )
    aggregated = (inv_root * gathered).astype(jnp.bfloat16)
    agg_full = lax.all_gather(aggregated, "cols", axis=1, tiled=True)
    pre = jnp.dot(agg_full, weight, preferred_element_type=jnp.float32)
    activation = jax.nn.silu(pre).astype(jnp.bfloat16)
    sigma = jax.nn.sigmoid(pre)
    grad_pre = (cotangent.astype(jnp.float32) * sigma * (1.0 + pre * (1.0 - sigma))).astype(
        jnp.bfloat16
    )
    partial_grad = lax.dot_general(
        agg_full, grad_pre, (((0,), (0,)), ((), ())), preferred_element_type=jnp.float32
    )
    weight_grad = lax.psum(partial_grad, "nodes")
    terms = lax.dot_general(
        grad_pre, weight, (((1,), (1,)), ((), ())), preferred_element_type=jnp.float32
    )
    grad_agg = lax.psum_scatter(terms, "cols", scatter_dimension=1, tiled=True)
    grad_scaled = (inv_root * grad_agg).astype(jnp.bfloat16)
    all_cols, all_counts, all_codes = (
        lax.all_gather(tile_cols, "nodes", axis=0, tiled=True),
        lax.all_gather(tile_count, "nodes", axis=0, tiled=True),
        lax.all_gather(tile_codes, "nodes", axis=0, tiled=True),
    )
    pieces = lax.all_gather(grad_scaled[None], "nodes", axis=0, tiled=True)
    count_blocks = pieces.shape[0]
    row_ids = jnp.arange(count_blocks, dtype=jnp.int32)
    tiles = make_tiles(all_cols == my_block, all_codes, all_counts, row_ids == my_block, identity)
    back_total = lax.dot_general(
        tiles, pieces, (((0, 1), (0, 1)), ((), ())), preferred_element_type=jnp.float32
    )
    feats_grad = inv_root * back_total
    return (activation, weight_grad, feats_grad)


FUSED_SHAPE = (8, 4)


def dot(a, b, dims):
    return lax.dot_general(a, b, (dims, ((), ())), preferred_element_type=jnp.float32)


def hash_tile(code, base):
    hashed = (code * 73856093) ^ base
    hashed = hashed ^ hashed >> 13
    hashed = hashed * 1274126177
    hashed = hashed ^ hashed >> 16
    present = jnp.where(code >= 0, 1.0, 0.0)
    return jnp.where(hashed & 63 == 0, present, 0.0).astype(jnp.bfloat16)


def fused_kernel(
    nodes, cols,
    features_hbm, weight_hbm, degree_hbm, tile_cols_hbm, tile_count_hbm, tile_codes_hbm, cotangent_hbm,
    activation, weight_grad, feats_grad,
    weight, degree, tile_cols, tile_count, tile_codes,
    x_all, cot_all, w_all, meta, base, base_t, eye, adj, adj_t, d_col, y_all, xt_out, xt_in, agg_t,
    pre, grad, u_all, wg_all,
    load_sem, x_send, x_recv, meta_send, meta_recv, cot_send, cot_recv, w_send, w_recv,
    y_send, y_recv, xt_send, xt_recv, u_send, u_recv, wg_send, wg_recv,
):
    n = lax.axis_index("nodes")
    c = lax.axis_index("cols")
    chips = nodes // 2
    chip, core = n // 2, lax.rem(n, 2)
    x_at = lax.rem(chip, 2)
    x_chip = chip + 1 - 2 * x_at
    y_chip = lax.rem(chip + 2, chips)
    far_chip = lax.rem(x_chip + 2, chips)
    other = 1 - core
    partner = 2 * chip + other
    x_twin, x_cross = 2 * x_chip + core, 2 * x_chip + other
    y_twin, y_cross = 2 * y_chip + core, 2 * y_chip + other
    far_twin, far_cross = 2 * far_chip + core, 2 * far_chip + other
    node_peers = [far_twin, x_twin, y_twin, x_cross, y_cross, far_cross, partner]
    col_peers = [lax.rem(c + d, cols) for d in range(1, cols)]

    barrier = pltpu.get_barrier_semaphore()
    for peer in node_peers:
        pl.semaphore_signal(barrier, inc=1, device_id=(peer, c), device_id_type=MESH)
    for peer in col_peers:
        pl.semaphore_signal(barrier, inc=1, device_id=(n, peer), device_id_type=MESH)

    loads = []
    for i, (src, dst) in enumerate((
        (tile_cols_hbm, tile_cols), (tile_count_hbm, tile_count), (tile_codes_hbm, tile_codes), (degree_hbm, degree),
        (features_hbm, x_all.at[c]), (weight_hbm, weight), (cotangent_hbm, cot_all.at[n]),
    )):
        loads.append(pltpu.make_async_copy(src, dst, load_sem.at[i]))
        loads[-1].start()

    sent = []

    def push(src, dst, peer, send, recv):
        copy = pltpu.make_async_remote_copy(
            src_ref=src, dst_ref=dst, send_sem=send, recv_sem=recv, device_id=peer, device_id_type=MESH
        )
        copy.start()
        sent.append(copy)
        return copy

    def push_nodes(src_of, dst, send, recv):
        return [
            push(src_of(peer), dst, (peer, c), send.at[i], recv.at[i])
            for i, peer in enumerate(node_peers)
        ]

    row_ids = lax.broadcasted_iota(jnp.int32, (TILE, TILE), 0)
    lane_ids = lax.broadcasted_iota(jnp.int32, (TILE, TILE), 1)
    eye[...] = jnp.where(row_ids == lane_ids, 1.0, 0.0)
    base[...] = row_ids * 19349663 ^ lane_ids * 83492791
    base_t[...] = lane_ids * 19349663 ^ row_ids * 83492791

    pl.semaphore_wait(barrier, nodes + cols - 2)

    x_copies = [
        push(features_hbm, x_all.at[c], (n, peer), x_send.at[i], x_recv.at[i])
        for i, peer in enumerate(col_peers)
    ]

    for load in loads[:4]:
        load.wait()
    for block in range(nodes):
        code = jnp.int32(-1)
        for slot in range(nodes):
            hit = (tile_cols[0, slot] == block) & (slot < tile_count[0, 0])
            code = jnp.where(hit, tile_codes[0, slot], code)
        meta[n, block] = jnp.full((1, TILE), code, jnp.int32)
    meta[n, nodes] = degree[...]
    meta_copies = push_nodes(lambda peer: meta.at[n], meta.at[n], meta_send, meta_recv)
    cot_copies = push_nodes(lambda peer: cotangent_hbm, cot_all.at[n], cot_send, cot_recv)

    def lanes(block):
        return pl.ds(pl.multiple_of(block * TILE, TILE), TILE)

    def make_row(row):
        inv_row = lax.rsqrt(meta[row, nodes].astype(jnp.float32))
        inv_col = jnp.sum(eye[...] * inv_row, axis=1, keepdims=True)
        d_col[lanes(row), :] = jnp.broadcast_to(inv_col, (TILE, TILE))
        for block in range(nodes):
            half = (block % 2) * TILE
            adj[block // 2, lanes(row), half:half + TILE] = hash_tile(meta[row, block], base[...])
        adj_t[:, lanes(row)] = hash_tile(meta[row, n], base_t[...])
        own = (row // 2, lanes(row), lanes(lax.rem(row, 2)))
        adj[own] = adj[own] + eye[...].astype(jnp.bfloat16)

    make_row(n)
    adj_t[:, lanes(n)] = adj_t[:, lanes(n)] + eye[...].astype(jnp.bfloat16)
    meta_copies[-1].wait_recv()
    make_row(partner)

    for load in loads[4:6]:
        load.wait()
    for copy in x_copies:
        copy.wait_recv()
    y = dot(x_all[0], weight[:TILE, :], ((1,), (0,)))
    for q in range(1, cols):
        y += dot(x_all[q], weight[q * TILE:(q + 1) * TILE, :], ((1,), (0,)))
    y_all[n] = (d_col[lanes(n), :] * y).astype(jnp.bfloat16)
    y_copies = [
        push(y_all.at[n], y_all.at[n], (peer, c), y_send.at[i], y_recv.at[i])
        for i, peer in enumerate((far_twin, x_twin, y_twin, x_cross, y_cross, partner))
    ]

    rows = xt_in.shape[1]
    for q in range(cols):
        turned = jnp.transpose(x_all[q].astype(jnp.float32)).astype(jnp.bfloat16)
        for i in range(TILE // rows):
            xt_out[q * (TILE // rows) + i] = turned[i * rows:(i + 1) * rows, :]
    xt_copies = push_nodes(lambda peer: xt_out.at[peer], xt_in.at[n], xt_send, xt_recv)
    xt_in[n] = xt_out[n]
    w_copies = [
        push(weight_hbm.at[lanes(peer), :], w_all.at[c], (n, peer), w_send.at[i], w_recv.at[i])
        for i, peer in enumerate(col_peers)
    ]
    w_all[c] = weight[lanes(c), :]

    for copy in meta_copies[:-1]:
        copy.wait_recv()

    def make_far(i, carry):
        make_row(lax.rem(2 * chip + i, nodes))
        return carry

    lax.fori_loop(2, nodes, make_far, 0)

    def block_pair(at):
        return y_all[pl.ds(2 * at, 2)].reshape(2 * TILE, TILE)

    y_copies[-1].wait_recv()
    pre[...] = dot(adj[chip], block_pair(chip), ((1,), (0,)))
    y_copies[0].wait_recv()
    relay = push(y_all.at[far_twin], y_all.at[far_twin], (partner, c), y_send.at[6], y_recv.at[6])
    y_copies[1].wait_recv()
    y_copies[3].wait_recv()
    pre[...] += dot(adj[x_chip], block_pair(x_chip), ((1,), (0,)))
    y_copies[2].wait_recv()
    y_copies[4].wait_recv()
    pre[...] += dot(adj[y_chip], block_pair(y_chip), ((1,), (0,)))
    loads[6].wait()
    for copy in cot_copies:
        copy.wait_recv()
    relay.wait_recv()
    last = block_pair(far_chip)
    u = jnp.zeros((TILE, TILE), jnp.float32)
    for i in range(chips):
        part = slice(2 * i * TILE, 2 * (i + 1) * TILE)
        inv_root = d_col[part, :]
        value = (pre[part, :] + dot(adj[far_chip, part, :], last, ((1,), (0,)))) * inv_root
        pre[part, :] = value
        sigma = 0.5 * jnp.tanh(0.5 * value) + 0.5
        cot = cot_all[2 * i:2 * i + 2].reshape(2 * TILE, TILE).astype(jnp.float32)
        grad[part, :] = (inv_root * (cot * sigma * (1.0 + value * (1.0 - sigma)))).astype(jnp.bfloat16)
        u += dot(adj_t[:, part], grad[part, :], ((1,), (0,)))
    u_all[c] = (d_col[lanes(n), :] * u).astype(jnp.bfloat16)
    u_copies = [
        push(u_all.at[c], u_all.at[c], (n, peer), u_send.at[i], u_recv.at[i])
        for i, peer in enumerate(col_peers)
    ]

    for copy in xt_copies:
        copy.wait_recv()
    total = jnp.zeros(agg_t.shape, jnp.float32)
    for i in range(chips):
        scaled = jnp.concatenate([
            (xt_in[block].astype(jnp.float32) * lax.rsqrt(meta[block, nodes].astype(jnp.float32))).astype(jnp.bfloat16)
            for block in (2 * i, 2 * i + 1)
        ], axis=1)
        total += dot(scaled, adj[i], ((1,), (1,)))
    agg_t[...] = total.astype(jnp.bfloat16)
    wg_all[n] = dot(agg_t[...], grad[...], ((1,), (0,))).astype(wg_all.dtype)
    wg_copies = push_nodes(lambda peer: wg_all.at[n], wg_all.at[n], wg_send, wg_recv)
    own = pre[lanes(n), :]
    activation[...] = (own * jax.nn.sigmoid(own)).astype(jnp.bfloat16)

    for copy in w_copies + u_copies:
        copy.wait_recv()
    out = dot(u_all[0], w_all[0], ((1,), (1,)))
    for q in range(1, cols):
        out += dot(u_all[q], w_all[q], ((1,), (1,)))
    feats_grad[...] = out

    for copy in wg_copies:
        copy.wait_recv()
    for block in range(nodes):
        weight_grad[block * rows:(block + 1) * rows, :] = wg_all[block].astype(jnp.float32)
    for copy in sent:
        copy.wait_send()


def write_out_kernel(*refs):
    count = len(refs) // 2
    copies = [pltpu.make_async_copy(refs[i], refs[count + i], refs[-1].at[i]) for i in range(count)]
    for copy in copies:
        copy.start()
    for copy in copies:
        copy.wait()


def fused(nodes, cols, features, weight, degree, tile_cols, tile_count, tile_codes, cotangent):
    rows = weight.shape[0] // nodes
    hbm = pl.BlockSpec(memory_space=pltpu.HBM)
    vmem = pl.BlockSpec(memory_space=pltpu.VMEM)
    block = (TILE, TILE)
    total = nodes * TILE
    outs = ((features.shape, jnp.bfloat16), (weight.shape, jnp.float32), (features.shape, jnp.float32))
    dma = pltpu.SemaphoreType.DMA
    results = pl.pallas_call(
        functools.partial(fused_kernel, nodes, cols),
        out_shape=tuple(pltpu.VMEM(shape, dtype) for shape, dtype in outs),
        in_specs=[hbm] * 7,
        out_specs=(vmem, vmem, vmem),
        scratch_shapes=[
            pltpu.VMEM(weight.shape, jnp.bfloat16),
            pltpu.VMEM((1, TILE), jnp.int32),
            pltpu.SMEM(tile_cols.shape, jnp.int32),
            pltpu.SMEM((1, 1), jnp.int32),
            pltpu.SMEM(tile_codes.shape, jnp.int32),
            pltpu.VMEM((cols,) + block, jnp.bfloat16),
            pltpu.VMEM((nodes,) + block, jnp.bfloat16),
            pltpu.VMEM((cols,) + block, jnp.bfloat16),
            pltpu.VMEM((nodes, nodes + 1, 1, TILE), jnp.int32),
            pltpu.VMEM(block, jnp.int32),
            pltpu.VMEM(block, jnp.int32),
            pltpu.VMEM(block, jnp.float32),
            pltpu.VMEM((nodes // 2, total, 2 * TILE), jnp.bfloat16),
            pltpu.VMEM((TILE, total), jnp.bfloat16),
            pltpu.VMEM((total, TILE), jnp.float32),
            pltpu.VMEM((nodes,) + block, jnp.bfloat16),
            pltpu.VMEM((nodes, rows, TILE), jnp.bfloat16),
            pltpu.VMEM((nodes, rows, TILE), jnp.bfloat16),
            pltpu.VMEM((rows, total), jnp.bfloat16),
            pltpu.VMEM((total, TILE), jnp.float32),
            pltpu.VMEM((total, TILE), jnp.bfloat16),
            pltpu.VMEM((cols,) + block, jnp.bfloat16),
            pltpu.VMEM((nodes, rows, TILE), jnp.bfloat16),
            dma((7,)),
            dma((cols - 1,)), dma((cols - 1,)),
            dma((nodes - 1,)), dma((nodes - 1,)),
            dma((nodes - 1,)), dma((nodes - 1,)),
            dma((cols - 1,)), dma((cols - 1,)),
            dma((nodes - 1,)), dma((nodes - 1,)),
            dma((nodes - 1,)), dma((nodes - 1,)),
            dma((cols - 1,)), dma((cols - 1,)),
            dma((nodes - 1,)), dma((nodes - 1,)),
        ],
        compiler_params=pltpu.CompilerParams(collective_id=0, has_side_effects=True),
        name="layer",
    )(features, weight, degree[None, :], tile_cols, tile_count[None, :], tile_codes, cotangent)
    return pl.pallas_call(
        write_out_kernel,
        out_shape=tuple(jax.ShapeDtypeStruct(shape, dtype) for shape, dtype in outs),
        in_specs=[vmem] * 3,
        out_specs=(pl.BlockSpec(memory_space=pl.ANY),) * 3,
        scratch_shapes=[dma((3,))],
        name="write_out",
    )(*[pltpu.with_memory_space_constraint(x, pltpu.VMEM) for x in results])


def solution(mesh):
    in_specs = (
        P("nodes", "cols"),
        P(None, "cols"),
        P("nodes"),
        P("nodes", None),
        P("nodes"),
        P("nodes", None),
        P("nodes", "cols"),
    )
    out_specs = (P("nodes", "cols"), P(None, "cols"), P("nodes", "cols"))
    local = body
    shape = (mesh.shape["nodes"], mesh.shape["cols"])
    if shape == FUSED_SHAPE:
        local = functools.partial(fused, *shape)
    return jax.shard_map(local, mesh=mesh, in_specs=in_specs, out_specs=out_specs, check_vma=False)
```

```python
import functools

import jax
import jax.numpy as jnp
from jax import lax
from jax.experimental import pallas as pl
from jax.experimental.pallas import tpu as pltpu
from jax.sharding import PartitionSpec as P

MESH = pl.DeviceIdType.MESH

TILE = 128


def tile_bits(pattern_code):
    line_ids = jnp.arange(TILE, dtype=jnp.int32)
    hashed = (
        pattern_code[..., None, None] * 73856093
        ^ line_ids[:, None] * 19349663
        ^ line_ids[None, :] * 83492791
    )
    hashed = hashed ^ hashed >> 13
    hashed = hashed * 1274126177
    hashed = hashed ^ hashed >> 16
    return hashed & 63 == 0


def make_tiles(matches, code_table, live_limit, own, identity):
    slot_ids = jnp.arange(matches.shape[1], dtype=jnp.int32)
    slot_index = jnp.sum(jnp.where(matches, slot_ids[None, :], 0), axis=1, dtype=jnp.int32)
    code_value = jnp.sum(jnp.where(matches, code_table, 0), axis=1, dtype=jnp.int32)
    pattern = tile_bits(code_value) & (slot_index < live_limit)[:, None, None]
    values = (
        pattern.astype(jnp.float32)
        + jnp.where(own, 1.0, 0.0).astype(jnp.float32)[:, None, None] * identity
    )
    return values.astype(jnp.bfloat16)


def body(features, weight, degree, tile_cols, tile_count, tile_codes, cotangent):
    my_block = lax.axis_index("nodes")
    identity = jnp.eye(TILE, dtype=jnp.float32)
    inv_root = lax.rsqrt(degree.astype(jnp.float32))[:, None]
    scaled = (features.astype(jnp.float32) * inv_root).astype(jnp.bfloat16)
    my_cols = tile_cols[0]
    my_codes = tile_codes[0]
    my_count = tile_count[0]
    pieces = lax.all_gather(scaled[None], "nodes", axis=0, tiled=True)
    count_blocks = pieces.shape[0]
    targets = jnp.arange(count_blocks, dtype=jnp.int32)
    matches = targets[:, None] == my_cols[None, :]
    tiles = make_tiles(matches, my_codes[None, :], my_count, targets == my_block, identity)
    gathered = lax.dot_general(
        tiles, pieces, (((0, 2), (0, 1)), ((), ())), preferred_element_type=jnp.float32
    )
    aggregated = (inv_root * gathered).astype(jnp.bfloat16)
    agg_full = lax.all_gather(aggregated, "cols", axis=1, tiled=True)
    pre = jnp.dot(agg_full, weight, preferred_element_type=jnp.float32)
    activation = jax.nn.silu(pre).astype(jnp.bfloat16)
    sigma = jax.nn.sigmoid(pre)
    grad_pre = (cotangent.astype(jnp.float32) * sigma * (1.0 + pre * (1.0 - sigma))).astype(
        jnp.bfloat16
    )
    partial_grad = lax.dot_general(
        agg_full, grad_pre, (((0,), (0,)), ((), ())), preferred_element_type=jnp.float32
    )
    weight_grad = lax.psum(partial_grad, "nodes")
    terms = lax.dot_general(
        grad_pre, weight, (((1,), (1,)), ((), ())), preferred_element_type=jnp.float32
    )
    grad_agg = lax.psum_scatter(terms, "cols", scatter_dimension=1, tiled=True)
    grad_scaled = (inv_root * grad_agg).astype(jnp.bfloat16)
    all_cols, all_counts, all_codes = (
        lax.all_gather(tile_cols, "nodes", axis=0, tiled=True),
        lax.all_gather(tile_count, "nodes", axis=0, tiled=True),
        lax.all_gather(tile_codes, "nodes", axis=0, tiled=True),
    )
    pieces = lax.all_gather(grad_scaled[None], "nodes", axis=0, tiled=True)
    count_blocks = pieces.shape[0]
    row_ids = jnp.arange(count_blocks, dtype=jnp.int32)
    tiles = make_tiles(all_cols == my_block, all_codes, all_counts, row_ids == my_block, identity)
    back_total = lax.dot_general(
        tiles, pieces, (((0, 1), (0, 1)), ((), ())), preferred_element_type=jnp.float32
    )
    feats_grad = inv_root * back_total
    return (activation, weight_grad, feats_grad)


FUSED_SHAPE = (8, 4)


def dot(a, b, dims):
    return lax.dot_general(a, b, (dims, ((), ())), preferred_element_type=jnp.float32)


def mul(a, b):
    return dot(a, b, ((1,), (0,)))


def turn(block):
    return jnp.transpose(block.astype(jnp.float32)).astype(jnp.bfloat16)


def hash_tile(code, base):
    hashed = (code * 73856093) ^ base
    hashed = hashed ^ hashed >> 13
    hashed = hashed * 1274126177
    hashed = hashed ^ hashed >> 16
    present = jnp.where(code >= 0, 1.0, 0.0)
    return jnp.where(hashed & 63 == 0, present, 0.0).astype(jnp.bfloat16)


def lanes(block):
    return pl.ds(pl.multiple_of(block * TILE, TILE), TILE)


def fused_kernel(
    nodes, cols,
    features_hbm, weight_hbm, degree_hbm, tile_cols_hbm, tile_count_hbm, tile_codes_hbm, cotangent_hbm,
    activation, weight_grad, feats_grad,
    features, weight, degree, tile_cols, tile_count, tile_codes, cotangent,
    x_all, x_in, w_turned, w_all, cot_out, cot_in, meta, base, base_t, eye, adj_t, adj_own,
    y_out, y_in, d_row, agg, pre, grad, act_out, act_all, u_out, u_all, wg_all,
    load_sem, x_send, x_recv, meta_send, meta_recv, cot_send, cot_recv, w_send, w_recv,
    y_send, y_recv, xt_send, xt_recv, u_send, u_recv, near_send, near_recv, wg_send, wg_recv,
):
    n = lax.axis_index("nodes")
    c = lax.axis_index("cols")
    chips = nodes // 2
    chip, core = n // 2, lax.rem(n, 2)
    x_chip = chip + 1 - 2 * lax.rem(chip, 2)
    y_chip = lax.rem(chip + 2, chips)
    far_chip = lax.rem(x_chip + 2, chips)
    other = 1 - core
    partner = 2 * chip + other
    node_peers = [
        (2 * far_chip + core, core), (2 * far_chip + other, other),
        (2 * x_chip + core, core), (2 * x_chip + other, other),
        (2 * y_chip + core, core), (2 * y_chip + other, other),
        (partner, other),
    ]
    col_peers = [lax.rem(c + d, cols) for d in range(1, cols)]
    half = TILE // 2

    barrier = pltpu.get_barrier_semaphore()
    greeted = [(n, peer) for peer in col_peers] + [(partner, peer) for peer in col_peers]
    greeted += [(peer, c) for peer, _ in node_peers]
    for peer in greeted:
        pl.semaphore_signal(barrier, inc=1, device_id=peer, device_id_type=MESH)

    loads = []
    for i, (src, dst) in enumerate((
        (features_hbm, features), (tile_cols_hbm, tile_cols), (tile_count_hbm, tile_count),
        (tile_codes_hbm, tile_codes), (degree_hbm, degree), (cotangent_hbm, cotangent), (weight_hbm, weight),
    )):
        loads.append(pltpu.make_async_copy(src, dst, load_sem.at[i]))
        loads[-1].start()

    sent = []

    def push(src, dst, peer, send, recv):
        copy = pltpu.make_async_remote_copy(
            src_ref=src, dst_ref=dst, send_sem=send, recv_sem=recv, device_id=peer, device_id_type=MESH
        )
        copy.start()
        sent.append(copy)
        return copy

    def push_nodes(src_of, dst, send, recv):
        return [
            push(src_of(peer, side), dst, (peer, c), send.at[i], recv.at[i])
            for i, (peer, side) in enumerate(node_peers)
        ]

    loads[0].wait()
    x_all[pl.ds(2 * c, 2)] = turn(features[...]).reshape(2, half, TILE)

    pl.semaphore_wait(barrier, len(greeted))

    x_copies = [
        push(x_all.at[pl.ds(2 * c, 2)], x_all.at[pl.ds(2 * c, 2)], (n, peer), x_send.at[i], x_recv.at[i])
        for i, peer in enumerate(col_peers)
    ]

    for load in loads[1:5]:
        load.wait()
    for block in range(nodes):
        code = jnp.int32(-1)
        for slot in range(nodes):
            hit = (tile_cols[0, slot] == block) & (slot < tile_count[0, 0])
            code = jnp.where(hit, tile_codes[0, slot], code)
        meta[n, block] = jnp.full((1, TILE), code, jnp.int32)
    meta[n, nodes] = degree[...]
    meta_copies = push_nodes(lambda peer, side: meta.at[n], meta.at[n], meta_send, meta_recv)
    loads[5].wait()
    cot_out[...] = turn(cotangent[...]).reshape(2, half, TILE)
    cot_copies = push_nodes(lambda peer, side: cot_out.at[side], cot_in.at[n], cot_send, cot_recv)
    cot_in[n] = cot_out[core]

    row_ids = lax.broadcasted_iota(jnp.int32, (TILE, TILE), 0)
    lane_ids = lax.broadcasted_iota(jnp.int32, (TILE, TILE), 1)
    eye[...] = jnp.where(row_ids == lane_ids, 1.0, 0.0).astype(jnp.bfloat16)
    base[...] = row_ids * 19349663 ^ lane_ids * 83492791
    base_t[...] = lane_ids * 19349663 ^ row_ids * 83492791
    loads[6].wait()
    for q in range(cols):
        w_turned[:, q * TILE:(q + 1) * TILE] = turn(weight[q * TILE:(q + 1) * TILE, :])
    w_all[c] = weight[lanes(c), :]

    def inv_row(row):
        return lax.rsqrt(meta[row, nodes].astype(jnp.float32))

    def make_row(row):
        d_row[:, lanes(row)] = inv_row(row)
        for block in range(nodes):
            at = (block % 2) * TILE
            adj_t[block // 2, at:at + TILE, lanes(row)] = hash_tile(meta[row, block], base_t[...])
        for side in range(2):
            at = side * TILE
            adj_own[lanes(row), at:at + TILE] = hash_tile(meta[row, 2 * chip + side], base[...])
        own = (row // 2, lanes(lax.rem(row, 2)), lanes(row))
        adj_t[own] = adj_t[own] + eye[...]

    make_row(n)
    meta_copies[-1].wait_recv()
    make_row(partner)
    for side in range(2):
        own = (lanes(2 * chip + side), slice(side * TILE, (side + 1) * TILE))
        adj_own[own] = adj_own[own] + eye[...]

    for copy in x_copies:
        copy.wait_recv()
    y = mul(w_turned[...], x_all[...].reshape(cols * TILE, TILE)) * inv_row(n)
    y_out[...] = y.astype(jnp.bfloat16).reshape(2, half, TILE)
    y_copies = push_nodes(lambda peer, side: y_out.at[side], y_in.at[n], y_send, y_recv)
    xt_copies = push_nodes(lambda peer, side: x_all.at[peer], x_in.at[n], xt_send, xt_recv)
    w_copies = [
        push(weight.at[lanes(peer), :], w_all.at[c], (n, peer), w_send.at[i], w_recv.at[i])
        for i, peer in enumerate(col_peers)
    ]
    y_in[n] = y_out[core]
    x_in[n] = x_all[n]

    for copy in meta_copies[:-1]:
        copy.wait_recv()

    def make_far(i, carry):
        make_row(lax.rem(2 * chip + i, nodes))
        return carry

    lax.fori_loop(2, nodes, make_far, 0)

    def chip_pair(buffer, at):
        return jnp.concatenate([buffer[2 * at], buffer[2 * at + 1]], axis=1)

    for copy in cot_copies:
        copy.wait_recv()
    y_copies[6].wait_recv()
    pre[...] = mul(chip_pair(y_in, chip), adj_t[chip])
    for copy in y_copies[2:6]:
        copy.wait_recv()
    pre[...] += mul(chip_pair(y_in, x_chip), adj_t[x_chip]) + mul(chip_pair(y_in, y_chip), adj_t[y_chip])
    for copy in y_copies[:2]:
        copy.wait_recv()
    inv = d_row[...]
    value = (pre[...] + mul(chip_pair(y_in, far_chip), adj_t[far_chip])) * inv
    pre[...] = value
    sigma = 0.5 * jnp.tanh(0.5 * value) + 0.5
    cot = jnp.concatenate([cot_in[block] for block in range(nodes)], axis=1).astype(jnp.float32)
    grad[core] = (inv * (cot * sigma * (1.0 + value * (1.0 - sigma)))).astype(jnp.bfloat16)
    u = mul(grad[core], adj_own[...])
    for side in range(2):
        u_out[side] = (u[:, side * TILE:(side + 1) * TILE] * inv_row(2 * chip + side)).astype(jnp.bfloat16)
    here = u_all.at[2 * c + core]
    u_copies = []
    for i, peer in enumerate(col_peers):
        u_copies.append(push(u_out.at[core], here, (n, peer), u_send.at[2 * i], u_recv.at[2 * i]))
        u_copies.append(push(u_out.at[other], here, (partner, peer), u_send.at[2 * i + 1], u_recv.at[2 * i + 1]))
    u_copies.append(push(u_out.at[other], here, (partner, c), u_send.at[2 * cols - 2], u_recv.at[2 * cols - 2]))
    u_all[2 * c + core] = u_out[core]

    grad_copy = push(grad.at[core], grad.at[core], (partner, c), near_send.at[0], near_recv.at[0])
    for side, block in enumerate((n, partner)):
        own = pre[:, lanes(block)]
        act_out[side] = (own * jax.nn.sigmoid(own)).astype(jnp.bfloat16)
    act_copy = push(act_out.at[1], act_all.at[core], (partner, c), near_send.at[1], near_recv.at[1])
    act_all[core] = act_out[0]

    for copy in xt_copies:
        copy.wait_recv()
    total = jnp.zeros(agg.shape, jnp.float32)
    for i in range(chips):
        scaled = jnp.concatenate([
            (x_in[block].astype(jnp.float32) * inv_row(block)).astype(jnp.bfloat16)
            for block in (2 * i, 2 * i + 1)
        ], axis=1)
        total += mul(scaled, adj_t[i])
    agg[...] = total.astype(jnp.bfloat16)
    grad_copy.wait_recv()
    wg_all[n] = dot(agg[...], grad[...].reshape(TILE, nodes * TILE), ((1,), (1,))).astype(wg_all.dtype)
    wg_copies = push_nodes(lambda peer, side: wg_all.at[n], wg_all.at[n], wg_send, wg_recv)
    act_copy.wait_recv()
    activation[...] = turn(act_all[...].reshape(TILE, TILE))

    for copy in w_copies + u_copies:
        copy.wait_recv()
    w_wide = jnp.concatenate([w_all[q] for q in range(cols)], axis=1)
    feats_grad[...] = jnp.transpose(mul(w_wide, u_all[...].reshape(cols * TILE, TILE)))

    for copy in wg_copies:
        copy.wait_recv()
    for block in range(nodes):
        weight_grad[block * half:(block + 1) * half, :] = wg_all[block].astype(jnp.float32)
    for copy in sent:
        copy.wait_send()


def write_out_kernel(*refs):
    count = len(refs) // 2
    copies = [pltpu.make_async_copy(refs[i], refs[count + i], refs[-1].at[i]) for i in range(count)]
    for copy in copies:
        copy.start()
    for copy in copies:
        copy.wait()


def fused(nodes, cols, features, weight, degree, tile_cols, tile_count, tile_codes, cotangent):
    hbm = pl.BlockSpec(memory_space=pltpu.HBM)
    vmem = pl.BlockSpec(memory_space=pltpu.VMEM)
    block = (TILE, TILE)
    halves = (TILE // 2, TILE)
    total = nodes * TILE
    outs = ((features.shape, jnp.bfloat16), (weight.shape, jnp.float32), (features.shape, jnp.float32))
    dma = pltpu.SemaphoreType.DMA
    results = pl.pallas_call(
        functools.partial(fused_kernel, nodes, cols),
        out_shape=tuple(pltpu.VMEM(shape, dtype) for shape, dtype in outs),
        in_specs=[hbm] * 7,
        out_specs=(vmem, vmem, vmem),
        scratch_shapes=[
            pltpu.VMEM(features.shape, jnp.bfloat16),
            pltpu.VMEM(weight.shape, jnp.bfloat16),
            pltpu.VMEM((1, TILE), jnp.int32),
            pltpu.SMEM(tile_cols.shape, jnp.int32),
            pltpu.SMEM((1, 1), jnp.int32),
            pltpu.SMEM(tile_codes.shape, jnp.int32),
            pltpu.VMEM(cotangent.shape, jnp.bfloat16),
            pltpu.VMEM((2 * cols,) + halves, jnp.bfloat16),
            pltpu.VMEM((nodes,) + halves, jnp.bfloat16),
            pltpu.VMEM((TILE, weight.shape[0]), jnp.bfloat16),
            pltpu.VMEM((cols,) + block, jnp.bfloat16),
            pltpu.VMEM((2,) + halves, jnp.bfloat16),
            pltpu.VMEM((nodes,) + halves, jnp.bfloat16),
            pltpu.VMEM((nodes, nodes + 1, 1, TILE), jnp.int32),
            pltpu.VMEM(block, jnp.int32),
            pltpu.VMEM(block, jnp.int32),
            pltpu.VMEM(block, jnp.bfloat16),
            pltpu.VMEM((nodes // 2, 2 * TILE, total), jnp.bfloat16),
            pltpu.VMEM((total, 2 * TILE), jnp.bfloat16),
            pltpu.VMEM((2,) + halves, jnp.bfloat16),
            pltpu.VMEM((nodes,) + halves, jnp.bfloat16),
            pltpu.VMEM((1, total), jnp.float32),
            pltpu.VMEM((TILE // 2, total), jnp.bfloat16),
            pltpu.VMEM((TILE // 2, total), jnp.float32),
            pltpu.VMEM((2, TILE // 2, total), jnp.bfloat16),
            pltpu.VMEM((2,) + halves, jnp.bfloat16),
            pltpu.VMEM((2,) + halves, jnp.bfloat16),
            pltpu.VMEM((2,) + halves, jnp.bfloat16),
            pltpu.VMEM((2 * cols,) + halves, jnp.bfloat16),
            pltpu.VMEM((nodes,) + halves, jnp.bfloat16),
            dma((7,)),
            dma((cols - 1,)), dma((cols - 1,)),
            dma((nodes - 1,)), dma((nodes - 1,)),
            dma((nodes - 1,)), dma((nodes - 1,)),
            dma((cols - 1,)), dma((cols - 1,)),
            dma((nodes - 1,)), dma((nodes - 1,)),
            dma((nodes - 1,)), dma((nodes - 1,)),
            dma((2 * cols - 1,)), dma((2 * cols - 1,)),
            dma((2,)), dma((2,)),
            dma((nodes - 1,)), dma((nodes - 1,)),
        ],
        compiler_params=pltpu.CompilerParams(collective_id=0, has_side_effects=True),
        name="layer",
    )(features, weight, degree[None, :], tile_cols, tile_count[None, :], tile_codes, cotangent)
    return pl.pallas_call(
        write_out_kernel,
        out_shape=tuple(jax.ShapeDtypeStruct(shape, dtype) for shape, dtype in outs),
        in_specs=[vmem] * 3,
        out_specs=(pl.BlockSpec(memory_space=pl.ANY),) * 3,
        scratch_shapes=[dma((3,))],
        name="write_out",
    )(*[pltpu.with_memory_space_constraint(x, pltpu.VMEM) for x in results])


def solution(mesh):
    in_specs = (
        P("nodes", "cols"),
        P(None, "cols"),
        P("nodes"),
        P("nodes", None),
        P("nodes"),
        P("nodes", None),
        P("nodes", "cols"),
    )
    out_specs = (P("nodes", "cols"), P(None, "cols"), P("nodes", "cols"))
    local = body
    shape = (mesh.shape["nodes"], mesh.shape["cols"])
    if shape == FUSED_SHAPE:
        local = functools.partial(fused, *shape)
    return jax.shard_map(local, mesh=mesh, in_specs=in_specs, out_specs=out_specs, check_vma=False)
```

```python
import functools

import jax
import jax.numpy as jnp
from jax import lax
from jax.experimental import pallas as pl
from jax.experimental.pallas import tpu as pltpu
from jax.sharding import PartitionSpec as P

MESH = pl.DeviceIdType.MESH

TILE = 128


def tile_bits(pattern_code):
    line_ids = jnp.arange(TILE, dtype=jnp.int32)
    hashed = (
        pattern_code[..., None, None] * 73856093
        ^ line_ids[:, None] * 19349663
        ^ line_ids[None, :] * 83492791
    )
    hashed = hashed ^ hashed >> 13
    hashed = hashed * 1274126177
    hashed = hashed ^ hashed >> 16
    return hashed & 63 == 0


def make_tiles(matches, code_table, live_limit, own, identity):
    slot_ids = jnp.arange(matches.shape[1], dtype=jnp.int32)
    slot_index = jnp.sum(jnp.where(matches, slot_ids[None, :], 0), axis=1, dtype=jnp.int32)
    code_value = jnp.sum(jnp.where(matches, code_table, 0), axis=1, dtype=jnp.int32)
    pattern = tile_bits(code_value) & (slot_index < live_limit)[:, None, None]
    values = (
        pattern.astype(jnp.float32)
        + jnp.where(own, 1.0, 0.0).astype(jnp.float32)[:, None, None] * identity
    )
    return values.astype(jnp.bfloat16)


def body(features, weight, degree, tile_cols, tile_count, tile_codes, cotangent):
    my_block = lax.axis_index("nodes")
    identity = jnp.eye(TILE, dtype=jnp.float32)
    inv_root = lax.rsqrt(degree.astype(jnp.float32))[:, None]
    scaled = (features.astype(jnp.float32) * inv_root).astype(jnp.bfloat16)
    my_cols = tile_cols[0]
    my_codes = tile_codes[0]
    my_count = tile_count[0]
    pieces = lax.all_gather(scaled[None], "nodes", axis=0, tiled=True)
    count_blocks = pieces.shape[0]
    targets = jnp.arange(count_blocks, dtype=jnp.int32)
    matches = targets[:, None] == my_cols[None, :]
    tiles = make_tiles(matches, my_codes[None, :], my_count, targets == my_block, identity)
    gathered = lax.dot_general(
        tiles, pieces, (((0, 2), (0, 1)), ((), ())), preferred_element_type=jnp.float32
    )
    aggregated = (inv_root * gathered).astype(jnp.bfloat16)
    agg_full = lax.all_gather(aggregated, "cols", axis=1, tiled=True)
    pre = jnp.dot(agg_full, weight, preferred_element_type=jnp.float32)
    activation = jax.nn.silu(pre).astype(jnp.bfloat16)
    sigma = jax.nn.sigmoid(pre)
    grad_pre = (cotangent.astype(jnp.float32) * sigma * (1.0 + pre * (1.0 - sigma))).astype(
        jnp.bfloat16
    )
    partial_grad = lax.dot_general(
        agg_full, grad_pre, (((0,), (0,)), ((), ())), preferred_element_type=jnp.float32
    )
    weight_grad = lax.psum(partial_grad, "nodes")
    terms = lax.dot_general(
        grad_pre, weight, (((1,), (1,)), ((), ())), preferred_element_type=jnp.float32
    )
    grad_agg = lax.psum_scatter(terms, "cols", scatter_dimension=1, tiled=True)
    grad_scaled = (inv_root * grad_agg).astype(jnp.bfloat16)
    all_cols, all_counts, all_codes = (
        lax.all_gather(tile_cols, "nodes", axis=0, tiled=True),
        lax.all_gather(tile_count, "nodes", axis=0, tiled=True),
        lax.all_gather(tile_codes, "nodes", axis=0, tiled=True),
    )
    pieces = lax.all_gather(grad_scaled[None], "nodes", axis=0, tiled=True)
    count_blocks = pieces.shape[0]
    row_ids = jnp.arange(count_blocks, dtype=jnp.int32)
    tiles = make_tiles(all_cols == my_block, all_codes, all_counts, row_ids == my_block, identity)
    back_total = lax.dot_general(
        tiles, pieces, (((0, 1), (0, 1)), ((), ())), preferred_element_type=jnp.float32
    )
    feats_grad = inv_root * back_total
    return (activation, weight_grad, feats_grad)


FUSED_SHAPE = (8, 4)


def dot(a, b, dims):
    return lax.dot_general(a, b, (dims, ((), ())), preferred_element_type=jnp.float32)


def mul(a, b):
    return dot(a, b, ((1,), (0,)))


def turn(block):
    return jnp.transpose(block.astype(jnp.float32)).astype(jnp.bfloat16)


def hash_tile(code, base):
    hashed = (code * 73856093) ^ base
    hashed = hashed ^ hashed >> 13
    hashed = hashed * 1274126177
    hashed = hashed ^ hashed >> 16
    present = jnp.where(code >= 0, 1.0, 0.0)
    return jnp.where(hashed & 63 == 0, present, 0.0).astype(jnp.bfloat16)


def lanes(block):
    return pl.ds(pl.multiple_of(block * TILE, TILE), TILE)


def fused_kernel(
    nodes, cols,
    features_hbm, weight_hbm, degree_hbm, tile_cols_hbm, tile_count_hbm, tile_codes_hbm, cotangent_hbm,
    activation, weight_grad, feats_grad,
    features, weight, degree, tile_cols, tile_count, tile_codes, cotangent,
    x_all, x_in, w_turned, w_all, cot_out, cot_in, meta, base, base_t, eye, adj_t, adj_own,
    y_out, y_in, d_row, agg, pre, grad, act_out, act_all, u_out, u_all, wg_all,
    load_sem, x_send, x_recv, meta_send, meta_recv, cot_send, cot_recv, w_send, w_recv,
    y_send, y_recv, xt_send, xt_recv, u_send, u_recv, near_send, near_recv, wg_send, wg_recv,
):
    n = lax.axis_index("nodes")
    c = lax.axis_index("cols")
    chips = nodes // 2
    chip, core = n // 2, lax.rem(n, 2)
    x_chip = chip + 1 - 2 * lax.rem(chip, 2)
    y_chip = lax.rem(chip + 2, chips)
    far_chip = lax.rem(x_chip + 2, chips)
    other = 1 - core
    partner = 2 * chip + other
    node_peers = [
        (2 * far_chip + core, core), (2 * far_chip + other, other),
        (2 * x_chip + core, core), (2 * x_chip + other, other),
        (2 * y_chip + core, core), (2 * y_chip + other, other),
        (partner, other),
    ]
    col_peers = [lax.rem(c + d, cols) for d in range(1, cols)]
    half = TILE // 2

    barrier = pltpu.get_barrier_semaphore()
    greeted = [(n, peer) for peer in col_peers] + [(partner, peer) for peer in col_peers]
    greeted += [(peer, c) for peer, _ in node_peers]
    for peer in greeted:
        pl.semaphore_signal(barrier, inc=1, device_id=peer, device_id_type=MESH)

    loads = []
    for i, (src, dst) in enumerate((
        (features_hbm, features), (tile_cols_hbm, tile_cols), (tile_count_hbm, tile_count),
        (tile_codes_hbm, tile_codes), (degree_hbm, degree), (cotangent_hbm, cotangent), (weight_hbm, weight),
    )):
        loads.append(pltpu.make_async_copy(src, dst, load_sem.at[i]))
        loads[-1].start()

    sent = []

    def push(src, dst, peer, send, recv):
        copy = pltpu.make_async_remote_copy(
            src_ref=src, dst_ref=dst, send_sem=send, recv_sem=recv, device_id=peer, device_id_type=MESH
        )
        copy.start()
        sent.append(copy)
        return copy

    def push_nodes(src_of, dst, send, recv):
        return [
            push(src_of(peer, side), dst, (peer, c), send.at[i], recv.at[i])
            for i, (peer, side) in enumerate(node_peers)
        ]

    loads[0].wait()
    x_all[pl.ds(2 * c, 2)] = turn(features[...]).reshape(2, half, TILE)

    pl.semaphore_wait(barrier, len(greeted))

    orders = ((3, 2, 1), (2, 3, 0), (3, 0, 1), (0, 1, 2))
    x_order = [sum(jnp.where(c == at, order[i], 0) for at, order in enumerate(orders)) for i in range(cols - 1)]
    x_copies = [
        push(x_all.at[pl.ds(2 * c, 2)], x_all.at[pl.ds(2 * c, 2)], (n, peer), x_send.at[i], x_recv.at[c])
        for i, peer in enumerate(x_order)
    ]

    for load in loads[1:5]:
        load.wait()
    for block in range(nodes):
        code = jnp.int32(-1)
        for slot in range(nodes):
            hit = (tile_cols[0, slot] == block) & (slot < tile_count[0, 0])
            code = jnp.where(hit, tile_codes[0, slot], code)
        meta[n, block] = jnp.full((1, TILE), code, jnp.int32)
    meta[n, nodes] = degree[...]
    meta_copies = push_nodes(lambda peer, side: meta.at[n], meta.at[n], meta_send, meta_recv)
    loads[5].wait()
    cot_out[...] = turn(cotangent[...]).reshape(2, half, TILE)
    cot_copies = push_nodes(lambda peer, side: cot_out.at[side], cot_in.at[n], cot_send, cot_recv)
    cot_in[n] = cot_out[core]

    row_ids = lax.broadcasted_iota(jnp.int32, (TILE, TILE), 0)
    lane_ids = lax.broadcasted_iota(jnp.int32, (TILE, TILE), 1)
    eye[...] = jnp.where(row_ids == lane_ids, 1.0, 0.0).astype(jnp.bfloat16)
    base[...] = row_ids * 19349663 ^ lane_ids * 83492791
    base_t[...] = lane_ids * 19349663 ^ row_ids * 83492791
    loads[6].wait()
    for q in range(cols):
        w_turned[:, q * TILE:(q + 1) * TILE] = turn(weight[q * TILE:(q + 1) * TILE, :])
    w_all[c] = weight[lanes(c), :]

    def inv_row(row):
        return lax.rsqrt(meta[row, nodes].astype(jnp.float32))

    def make_row(row):
        d_row[:, lanes(row)] = inv_row(row)
        for block in range(nodes):
            at = (block % 2) * TILE
            adj_t[block // 2, at:at + TILE, lanes(row)] = hash_tile(meta[row, block], base_t[...])
        for side in range(2):
            at = side * TILE
            adj_own[lanes(row), at:at + TILE] = hash_tile(meta[row, 2 * chip + side], base[...])
        own = (row // 2, lanes(lax.rem(row, 2)), lanes(row))
        adj_t[own] = adj_t[own] + eye[...]

    make_row(n)
    meta_copies[-1].wait_recv()
    make_row(partner)
    for side in range(2):
        own = (lanes(2 * chip + side), slice(side * TILE, (side + 1) * TILE))
        adj_own[own] = adj_own[own] + eye[...]

    for peer in col_peers:
        pltpu.make_async_copy(x_all.at[pl.ds(2 * peer, 2)], x_all.at[pl.ds(2 * peer, 2)], x_recv.at[peer]).wait()
    y = mul(w_turned[...], x_all[...].reshape(cols * TILE, TILE)) * inv_row(n)
    y_out[...] = y.astype(jnp.bfloat16).reshape(2, half, TILE)
    y_copies = push_nodes(lambda peer, side: y_out.at[side], y_in.at[n], y_send, y_recv)
    xt_copies = push_nodes(lambda peer, side: x_all.at[peer], x_in.at[n], xt_send, xt_recv)
    w_copies = [
        push(weight.at[lanes(peer), :], w_all.at[c], (n, peer), w_send.at[i], w_recv.at[i])
        for i, peer in enumerate(col_peers)
    ]
    y_in[n] = y_out[core]
    x_in[n] = x_all[n]

    for copy in meta_copies[:-1]:
        copy.wait_recv()

    def make_far(i, carry):
        make_row(lax.rem(2 * chip + i, nodes))
        return carry

    lax.fori_loop(2, nodes, make_far, 0)

    def chip_pair(buffer, at):
        return jnp.concatenate([buffer[2 * at], buffer[2 * at + 1]], axis=1)

    for copy in cot_copies:
        copy.wait_recv()
    y_copies[6].wait_recv()
    pre[...] = mul(chip_pair(y_in, chip), adj_t[chip])
    for copy in y_copies[2:6]:
        copy.wait_recv()
    pre[...] += mul(chip_pair(y_in, x_chip), adj_t[x_chip]) + mul(chip_pair(y_in, y_chip), adj_t[y_chip])
    for copy in y_copies[:2]:
        copy.wait_recv()
    inv = d_row[...]
    value = (pre[...] + mul(chip_pair(y_in, far_chip), adj_t[far_chip])) * inv
    pre[...] = value
    sigma = 0.5 * jnp.tanh(0.5 * value) + 0.5
    cot = jnp.concatenate([cot_in[block] for block in range(nodes)], axis=1).astype(jnp.float32)
    grad[core] = (inv * (cot * sigma * (1.0 + value * (1.0 - sigma)))).astype(jnp.bfloat16)
    u = mul(grad[core], adj_own[...])
    for side in range(2):
        u_out[side] = (u[:, side * TILE:(side + 1) * TILE] * inv_row(2 * chip + side)).astype(jnp.bfloat16)
    here = u_all.at[2 * c + core]
    u_copies = []
    for i, peer in enumerate(col_peers):
        u_copies.append(push(u_out.at[core], here, (n, peer), u_send.at[2 * i], u_recv.at[2 * i]))
        u_copies.append(push(u_out.at[other], here, (partner, peer), u_send.at[2 * i + 1], u_recv.at[2 * i + 1]))
    u_copies.append(push(u_out.at[other], here, (partner, c), u_send.at[2 * cols - 2], u_recv.at[2 * cols - 2]))
    u_all[2 * c + core] = u_out[core]

    grad_copy = push(grad.at[core], grad.at[core], (partner, c), near_send.at[0], near_recv.at[0])
    for side, block in enumerate((n, partner)):
        own = pre[:, lanes(block)]
        act_out[side] = (own * jax.nn.sigmoid(own)).astype(jnp.bfloat16)
    act_copy = push(act_out.at[1], act_all.at[core], (partner, c), near_send.at[1], near_recv.at[1])
    act_all[core] = act_out[0]

    for copy in xt_copies:
        copy.wait_recv()
    scaled = jnp.concatenate([
        (x_in[block].astype(jnp.float32) * inv_row(block)).astype(jnp.bfloat16) for block in range(nodes)
    ], axis=1)
    for i in range(chips):
        part = slice(2 * i * TILE, 2 * (i + 1) * TILE)
        agg[:, part] = mul(scaled, adj_t[:, :, part].reshape(nodes * TILE, 2 * TILE)).astype(jnp.bfloat16)
    grad_copy.wait_recv()
    wg_all[n] = dot(agg[...], grad[...].reshape(TILE, nodes * TILE), ((1,), (1,))).astype(wg_all.dtype)
    wg_copies = push_nodes(lambda peer, side: wg_all.at[n], wg_all.at[n], wg_send, wg_recv)
    act_copy.wait_recv()
    activation[...] = turn(act_all[...].reshape(TILE, TILE))

    for copy in sent[:-len(wg_copies)]:
        copy.wait_send()
    def term(q):
        return mul(w_all[q], u_all[pl.ds(2 * q, 2)].reshape(TILE, TILE))

    for copy in w_copies + u_copies[-1:]:
        copy.wait_recv()
    out = term(c)
    for d in range(1, cols):
        for copy in u_copies[2 * d - 2:2 * d]:
            copy.wait_recv()
        out += term(lax.rem(c + cols - d, cols))
    feats_grad[...] = jnp.transpose(out)

    for copy in wg_copies:
        copy.wait_recv()
    for block in range(nodes):
        weight_grad[block * half:(block + 1) * half, :] = wg_all[block].astype(jnp.float32)
    for copy in wg_copies:
        copy.wait_send()


def write_out_kernel(*refs):
    count = len(refs) // 2
    copies = [pltpu.make_async_copy(refs[i], refs[count + i], refs[-1].at[i]) for i in range(count)]
    for copy in copies:
        copy.start()
    for copy in copies:
        copy.wait()


def fused(nodes, cols, features, weight, degree, tile_cols, tile_count, tile_codes, cotangent):
    hbm = pl.BlockSpec(memory_space=pltpu.HBM)
    vmem = pl.BlockSpec(memory_space=pltpu.VMEM)
    block = (TILE, TILE)
    halves = (TILE // 2, TILE)
    total = nodes * TILE
    outs = ((features.shape, jnp.bfloat16), (weight.shape, jnp.float32), (features.shape, jnp.float32))
    dma = pltpu.SemaphoreType.DMA
    results = pl.pallas_call(
        functools.partial(fused_kernel, nodes, cols),
        out_shape=tuple(pltpu.VMEM(shape, dtype) for shape, dtype in outs),
        in_specs=[hbm] * 7,
        out_specs=(vmem, vmem, vmem),
        scratch_shapes=[
            pltpu.VMEM(features.shape, jnp.bfloat16),
            pltpu.VMEM(weight.shape, jnp.bfloat16),
            pltpu.VMEM((1, TILE), jnp.int32),
            pltpu.SMEM(tile_cols.shape, jnp.int32),
            pltpu.SMEM((1, 1), jnp.int32),
            pltpu.SMEM(tile_codes.shape, jnp.int32),
            pltpu.VMEM(cotangent.shape, jnp.bfloat16),
            pltpu.VMEM((2 * cols,) + halves, jnp.bfloat16),
            pltpu.VMEM((nodes,) + halves, jnp.bfloat16),
            pltpu.VMEM((TILE, weight.shape[0]), jnp.bfloat16),
            pltpu.VMEM((cols,) + block, jnp.bfloat16),
            pltpu.VMEM((2,) + halves, jnp.bfloat16),
            pltpu.VMEM((nodes,) + halves, jnp.bfloat16),
            pltpu.VMEM((nodes, nodes + 1, 1, TILE), jnp.int32),
            pltpu.VMEM(block, jnp.int32),
            pltpu.VMEM(block, jnp.int32),
            pltpu.VMEM(block, jnp.bfloat16),
            pltpu.VMEM((nodes // 2, 2 * TILE, total), jnp.bfloat16),
            pltpu.VMEM((total, 2 * TILE), jnp.bfloat16),
            pltpu.VMEM((2,) + halves, jnp.bfloat16),
            pltpu.VMEM((nodes,) + halves, jnp.bfloat16),
            pltpu.VMEM((1, total), jnp.float32),
            pltpu.VMEM((TILE // 2, total), jnp.bfloat16),
            pltpu.VMEM((TILE // 2, total), jnp.float32),
            pltpu.VMEM((2, TILE // 2, total), jnp.bfloat16),
            pltpu.VMEM((2,) + halves, jnp.bfloat16),
            pltpu.VMEM((2,) + halves, jnp.bfloat16),
            pltpu.VMEM((2,) + halves, jnp.bfloat16),
            pltpu.VMEM((2 * cols,) + halves, jnp.bfloat16),
            pltpu.VMEM((nodes,) + halves, jnp.bfloat16),
            dma((7,)),
            dma((cols - 1,)), dma((cols,)),
            dma((nodes - 1,)), dma((nodes - 1,)),
            dma((nodes - 1,)), dma((nodes - 1,)),
            dma((cols - 1,)), dma((cols,)),
            dma((nodes - 1,)), dma((nodes - 1,)),
            dma((nodes - 1,)), dma((nodes - 1,)),
            dma((2 * cols - 1,)), dma((2 * cols - 1,)),
            dma((2,)), dma((2,)),
            dma((nodes - 1,)), dma((nodes - 1,)),
        ],
        compiler_params=pltpu.CompilerParams(collective_id=0, has_side_effects=True),
        name="layer",
    )(features, weight, degree[None, :], tile_cols, tile_count[None, :], tile_codes, cotangent)
    return pl.pallas_call(
        write_out_kernel,
        out_shape=tuple(jax.ShapeDtypeStruct(shape, dtype) for shape, dtype in outs),
        in_specs=[vmem] * 3,
        out_specs=(pl.BlockSpec(memory_space=pl.ANY),) * 3,
        scratch_shapes=[dma((3,))],
        name="write_out",
    )(*[pltpu.with_memory_space_constraint(x, pltpu.VMEM) for x in results])


def solution(mesh):
    in_specs = (
        P("nodes", "cols"),
        P(None, "cols"),
        P("nodes"),
        P("nodes", None),
        P("nodes"),
        P("nodes", None),
        P("nodes", "cols"),
    )
    out_specs = (P("nodes", "cols"), P(None, "cols"), P("nodes", "cols"))
    local = body
    shape = (mesh.shape["nodes"], mesh.shape["cols"])
    if shape == FUSED_SHAPE:
        local = functools.partial(fused, *shape)
    return jax.shard_map(local, mesh=mesh, in_specs=in_specs, out_specs=out_specs, check_vma=False)
```

```python
import functools

import jax
import jax.numpy as jnp
from jax import lax
from jax.experimental import pallas as pl
from jax.experimental.pallas import tpu as pltpu
from jax.sharding import PartitionSpec as P

MESH = pl.DeviceIdType.MESH

TILE = 128


def tile_bits(pattern_code):
    line_ids = jnp.arange(TILE, dtype=jnp.int32)
    hashed = (
        pattern_code[..., None, None] * 73856093
        ^ line_ids[:, None] * 19349663
        ^ line_ids[None, :] * 83492791
    )
    hashed = hashed ^ hashed >> 13
    hashed = hashed * 1274126177
    hashed = hashed ^ hashed >> 16
    return hashed & 63 == 0


def make_tiles(matches, code_table, live_limit, own, identity):
    slot_ids = jnp.arange(matches.shape[1], dtype=jnp.int32)
    slot_index = jnp.sum(jnp.where(matches, slot_ids[None, :], 0), axis=1, dtype=jnp.int32)
    code_value = jnp.sum(jnp.where(matches, code_table, 0), axis=1, dtype=jnp.int32)
    pattern = tile_bits(code_value) & (slot_index < live_limit)[:, None, None]
    values = (
        pattern.astype(jnp.float32)
        + jnp.where(own, 1.0, 0.0).astype(jnp.float32)[:, None, None] * identity
    )
    return values.astype(jnp.bfloat16)


def body(features, weight, degree, tile_cols, tile_count, tile_codes, cotangent):
    my_block = lax.axis_index("nodes")
    identity = jnp.eye(TILE, dtype=jnp.float32)
    inv_root = lax.rsqrt(degree.astype(jnp.float32))[:, None]
    scaled = (features.astype(jnp.float32) * inv_root).astype(jnp.bfloat16)
    my_cols = tile_cols[0]
    my_codes = tile_codes[0]
    my_count = tile_count[0]
    pieces = lax.all_gather(scaled[None], "nodes", axis=0, tiled=True)
    count_blocks = pieces.shape[0]
    targets = jnp.arange(count_blocks, dtype=jnp.int32)
    matches = targets[:, None] == my_cols[None, :]
    tiles = make_tiles(matches, my_codes[None, :], my_count, targets == my_block, identity)
    gathered = lax.dot_general(
        tiles, pieces, (((0, 2), (0, 1)), ((), ())), preferred_element_type=jnp.float32
    )
    aggregated = (inv_root * gathered).astype(jnp.bfloat16)
    agg_full = lax.all_gather(aggregated, "cols", axis=1, tiled=True)
    pre = jnp.dot(agg_full, weight, preferred_element_type=jnp.float32)
    activation = jax.nn.silu(pre).astype(jnp.bfloat16)
    sigma = jax.nn.sigmoid(pre)
    grad_pre = (cotangent.astype(jnp.float32) * sigma * (1.0 + pre * (1.0 - sigma))).astype(
        jnp.bfloat16
    )
    partial_grad = lax.dot_general(
        agg_full, grad_pre, (((0,), (0,)), ((), ())), preferred_element_type=jnp.float32
    )
    weight_grad = lax.psum(partial_grad, "nodes")
    terms = lax.dot_general(
        grad_pre, weight, (((1,), (1,)), ((), ())), preferred_element_type=jnp.float32
    )
    grad_agg = lax.psum_scatter(terms, "cols", scatter_dimension=1, tiled=True)
    grad_scaled = (inv_root * grad_agg).astype(jnp.bfloat16)
    all_cols, all_counts, all_codes = (
        lax.all_gather(tile_cols, "nodes", axis=0, tiled=True),
        lax.all_gather(tile_count, "nodes", axis=0, tiled=True),
        lax.all_gather(tile_codes, "nodes", axis=0, tiled=True),
    )
    pieces = lax.all_gather(grad_scaled[None], "nodes", axis=0, tiled=True)
    count_blocks = pieces.shape[0]
    row_ids = jnp.arange(count_blocks, dtype=jnp.int32)
    tiles = make_tiles(all_cols == my_block, all_codes, all_counts, row_ids == my_block, identity)
    back_total = lax.dot_general(
        tiles, pieces, (((0, 1), (0, 1)), ((), ())), preferred_element_type=jnp.float32
    )
    feats_grad = inv_root * back_total
    return (activation, weight_grad, feats_grad)


FUSED_SHAPE = (8, 4)

X, META, COT, W, Y, XT, U, WG, GRAD, ACT, META_NEAR, Y_NEAR, Y_FAR = range(13)


def dot(a, b, dims):
    return lax.dot_general(a, b, (dims, ((), ())), preferred_element_type=jnp.float32)


def mul(a, b):
    return dot(a, b, ((1,), (0,)))


def turn(block):
    return jnp.transpose(block.astype(jnp.float32)).astype(jnp.bfloat16)


def hash_tile(code, base):
    hashed = (code * 73856093) ^ base
    hashed = hashed ^ hashed >> 13
    hashed = hashed * 1274126177
    hashed = hashed ^ hashed >> 16
    present = jnp.where(code >= 0, 1.0, 0.0)
    return jnp.where(hashed & 63 == 0, present, 0.0).astype(jnp.bfloat16)


def lanes(block):
    return pl.ds(pl.multiple_of(block * TILE, TILE), TILE)


def fused_kernel(
    nodes, cols,
    features_hbm, weight_hbm, degree_hbm, tile_cols_hbm, tile_count_hbm, tile_codes_hbm, cotangent_hbm,
    activation, weight_grad, feats_grad,
    features, weight, degree, tile_cols, tile_count, tile_codes, cotangent,
    x_all, x_in, w_turned, w_all, cot_out, cot_in, meta, base, base_t, eye, adj_t, adj_own,
    y_out, y_in, d_row, agg, pre, grad, act_out, act_all, u_out, u_all, wg_all,
    load_sem, send_sem, recv_sem,
):
    n = lax.axis_index("nodes")
    c = lax.axis_index("cols")
    chips = nodes // 2
    chip, core = n // 2, lax.rem(n, 2)
    x_chip = chip + 1 - 2 * lax.rem(chip, 2)
    y_chip = lax.rem(chip + 2, chips)
    far_chip = lax.rem(x_chip + 2, chips)
    other = 1 - core
    partner = 2 * chip + other
    node_peers = [
        (2 * far_chip + core, core), (2 * far_chip + other, other),
        (2 * x_chip + core, core), (2 * x_chip + other, other),
        (2 * y_chip + core, core), (2 * y_chip + other, other),
        (partner, other),
    ]
    col_peers = [lax.rem(c + d, cols) for d in range(1, cols)]
    half = TILE // 2

    barrier = pltpu.get_barrier_semaphore()
    greeted = [(n, peer) for peer in col_peers] + [(partner, peer) for peer in col_peers]
    greeted += [(peer, c) for peer, _ in node_peers]
    for peer in greeted:
        pl.semaphore_signal(barrier, inc=1, device_id=peer, device_id_type=MESH)

    loads = []
    for i, (src, dst) in enumerate((
        (features_hbm, features), (tile_cols_hbm, tile_cols), (tile_count_hbm, tile_count),
        (tile_codes_hbm, tile_codes), (degree_hbm, degree), (cotangent_hbm, cotangent), (weight_hbm, weight),
    )):
        loads.append(pltpu.make_async_copy(src, dst, load_sem.at[i]))
        loads[-1].start()

    def push(src, dst, peer, send, recv=None):
        pltpu.make_async_remote_copy(
            src_ref=src, dst_ref=dst, send_sem=send_sem.at[send], recv_sem=recv_sem.at[send if recv is None else recv],
            device_id=peer, device_id_type=MESH,
        ).start()

    def push_nodes(src_of, dst, send, far, near):
        recv = [far, far, send, send, send, send, near]
        for i, (peer, side) in enumerate(node_peers):
            push(src_of(peer, side), dst, (peer, c), send, recv[i])

    def wait_for(like, count, sem):
        whole = like if count == 0 else like.at[pl.ds(0, count)]
        pltpu.make_async_copy(whole, whole, sem).wait()

    def landed(like, count, recv):
        wait_for(like, count, recv_sem.at[recv])

    def left(like, count, send):
        wait_for(like, count, send_sem.at[send])

    loads[0].wait()
    x_all[pl.ds(2 * c, 2)] = turn(features[...]).reshape(2, half, TILE)

    pl.semaphore_wait(barrier, len(greeted))

    orders = ((3, 2, 1), (2, 3, 0), (3, 0, 1), (0, 1, 2))
    x_order = [sum(jnp.where(c == at, order[i], 0) for at, order in enumerate(orders)) for i in range(cols - 1)]
    for peer in x_order:
        push(x_all.at[pl.ds(2 * c, 2)], x_all.at[pl.ds(2 * c, 2)], (n, peer), X)

    for load in loads[1:5]:
        load.wait()
    for block in range(nodes):
        code = jnp.int32(-1)
        for slot in range(nodes):
            hit = (tile_cols[0, slot] == block) & (slot < tile_count[0, 0])
            code = jnp.where(hit, tile_codes[0, slot], code)
        meta[n, block] = jnp.full((1, TILE), code, jnp.int32)
    meta[n, nodes] = degree[...]
    push_nodes(lambda peer, side: meta.at[n], meta.at[n], META, META, META_NEAR)
    loads[5].wait()
    cot_out[...] = turn(cotangent[...]).reshape(2, half, TILE)
    push_nodes(lambda peer, side: cot_out.at[side], cot_in.at[n], COT, COT, COT)
    cot_in[n] = cot_out[core]

    row_ids = lax.broadcasted_iota(jnp.int32, (TILE, TILE), 0)
    lane_ids = lax.broadcasted_iota(jnp.int32, (TILE, TILE), 1)
    eye[...] = jnp.where(row_ids == lane_ids, 1.0, 0.0).astype(jnp.bfloat16)
    base[...] = row_ids * 19349663 ^ lane_ids * 83492791
    base_t[...] = lane_ids * 19349663 ^ row_ids * 83492791
    loads[6].wait()
    for q in range(cols):
        w_turned[:, q * TILE:(q + 1) * TILE] = turn(weight[q * TILE:(q + 1) * TILE, :])
    w_all[c] = weight[lanes(c), :]

    def inv_row(row):
        return lax.rsqrt(meta[row, nodes].astype(jnp.float32))

    def make_row(row):
        d_row[:, lanes(row)] = inv_row(row)
        for block in range(nodes):
            at = (block % 2) * TILE
            adj_t[block // 2, at:at + TILE, lanes(row)] = hash_tile(meta[row, block], base_t[...])
        for side in range(2):
            at = side * TILE
            adj_own[lanes(row), at:at + TILE] = hash_tile(meta[row, 2 * chip + side], base[...])
        own = (row // 2, lanes(lax.rem(row, 2)), lanes(row))
        adj_t[own] = adj_t[own] + eye[...]

    make_row(n)
    landed(meta, 1, META_NEAR)
    make_row(partner)
    for side in range(2):
        own = (lanes(2 * chip + side), slice(side * TILE, (side + 1) * TILE))
        adj_own[own] = adj_own[own] + eye[...]

    landed(x_all, 2 * (cols - 1), X)
    y = mul(w_turned[...], x_all[...].reshape(cols * TILE, TILE)) * inv_row(n)
    y_out[...] = y.astype(jnp.bfloat16).reshape(2, half, TILE)
    push_nodes(lambda peer, side: y_out.at[side], y_in.at[n], Y, Y_FAR, Y_NEAR)
    push_nodes(lambda peer, side: x_all.at[peer], x_in.at[n], XT, XT, XT)
    for peer in col_peers:
        push(weight.at[lanes(peer), :], w_all.at[c], (n, peer), W)
    y_in[n] = y_out[core]
    x_in[n] = x_all[n]

    landed(meta, nodes - 2, META)

    def make_far(i, carry):
        make_row(lax.rem(2 * chip + i, nodes))
        return carry

    lax.fori_loop(2, nodes, make_far, 0)

    def chip_pair(buffer, at):
        return jnp.concatenate([buffer[2 * at], buffer[2 * at + 1]], axis=1)

    landed(cot_in, nodes - 1, COT)
    landed(y_in, 1, Y_NEAR)
    pre[...] = mul(chip_pair(y_in, chip), adj_t[chip])
    landed(y_in, 4, Y)
    pre[...] += mul(chip_pair(y_in, x_chip), adj_t[x_chip]) + mul(chip_pair(y_in, y_chip), adj_t[y_chip])
    landed(y_in, 2, Y_FAR)
    inv = d_row[...]
    value = (pre[...] + mul(chip_pair(y_in, far_chip), adj_t[far_chip])) * inv
    pre[...] = value
    sigma = 0.5 * jnp.tanh(0.5 * value) + 0.5
    cot = jnp.concatenate([cot_in[block] for block in range(nodes)], axis=1).astype(jnp.float32)
    grad[core] = (inv * (cot * sigma * (1.0 + value * (1.0 - sigma)))).astype(jnp.bfloat16)
    u = mul(grad[core], adj_own[...])
    for side in range(2):
        u_out[side] = (u[:, side * TILE:(side + 1) * TILE] * inv_row(2 * chip + side)).astype(jnp.bfloat16)
    here = u_all.at[2 * c + core]
    for peer in col_peers:
        push(u_out.at[core], here, (n, peer), U)
        push(u_out.at[other], here, (partner, peer), U)
    push(u_out.at[other], here, (partner, c), U)
    u_all[2 * c + core] = u_out[core]

    push(grad.at[core], grad.at[core], (partner, c), GRAD)
    for side, block in enumerate((n, partner)):
        own = pre[:, lanes(block)]
        act_out[side] = (own * jax.nn.sigmoid(own)).astype(jnp.bfloat16)
    push(act_out.at[1], act_all.at[core], (partner, c), ACT)
    act_all[core] = act_out[0]

    landed(x_in, nodes - 1, XT)
    scaled = jnp.concatenate([
        (x_in[block].astype(jnp.float32) * inv_row(block)).astype(jnp.bfloat16) for block in range(nodes)
    ], axis=1)
    for i in range(chips):
        part = slice(2 * i * TILE, 2 * (i + 1) * TILE)
        agg[:, part] = mul(scaled, adj_t[:, :, part].reshape(nodes * TILE, 2 * TILE)).astype(jnp.bfloat16)
    landed(grad, 1, GRAD)
    wg_all[n] = dot(agg[...], grad[...].reshape(TILE, nodes * TILE), ((1,), (1,))).astype(wg_all.dtype)
    push_nodes(lambda peer, side: wg_all.at[n], wg_all.at[n], WG, WG, WG)
    landed(act_all, 1, ACT)
    activation[...] = turn(act_all[...].reshape(TILE, TILE))

    left(x_all, 2 * (cols - 1), X)
    left(meta, nodes - 1, META)
    left(cot_in, nodes - 1, COT)
    left(w_all, cols - 1, W)
    left(y_in, nodes - 1, Y)
    left(x_in, nodes - 1, XT)
    left(u_all, nodes - 1, U)
    left(grad, 1, GRAD)
    left(act_all, 1, ACT)
    landed(w_all, cols - 1, W)
    landed(u_all, 2 * cols - 1, U)
    w_wide = jnp.concatenate([w_all[q] for q in range(cols)], axis=1)
    feats_grad[...] = jnp.transpose(mul(w_wide, u_all[...].reshape(cols * TILE, TILE)))

    landed(wg_all, nodes - 1, WG)
    for block in range(nodes):
        weight_grad[block * half:(block + 1) * half, :] = wg_all[block].astype(jnp.float32)
    left(wg_all, nodes - 1, WG)


def write_out_kernel(*refs):
    count = len(refs) // 2
    copies = [pltpu.make_async_copy(refs[i], refs[count + i], refs[-1].at[i]) for i in range(count)]
    for copy in copies:
        copy.start()
    for copy in copies:
        copy.wait()


def fused(nodes, cols, features, weight, degree, tile_cols, tile_count, tile_codes, cotangent):
    hbm = pl.BlockSpec(memory_space=pltpu.HBM)
    vmem = pl.BlockSpec(memory_space=pltpu.VMEM)
    block = (TILE, TILE)
    halves = (TILE // 2, TILE)
    total = nodes * TILE
    outs = ((features.shape, jnp.bfloat16), (weight.shape, jnp.float32), (features.shape, jnp.float32))
    dma = pltpu.SemaphoreType.DMA
    results = pl.pallas_call(
        functools.partial(fused_kernel, nodes, cols),
        out_shape=tuple(pltpu.VMEM(shape, dtype) for shape, dtype in outs),
        in_specs=[hbm] * 7,
        out_specs=(vmem, vmem, vmem),
        scratch_shapes=[
            pltpu.VMEM(features.shape, jnp.bfloat16),
            pltpu.VMEM(weight.shape, jnp.bfloat16),
            pltpu.VMEM((1, TILE), jnp.int32),
            pltpu.SMEM(tile_cols.shape, jnp.int32),
            pltpu.SMEM((1, 1), jnp.int32),
            pltpu.SMEM(tile_codes.shape, jnp.int32),
            pltpu.VMEM(cotangent.shape, jnp.bfloat16),
            pltpu.VMEM((2 * cols,) + halves, jnp.bfloat16),
            pltpu.VMEM((nodes,) + halves, jnp.bfloat16),
            pltpu.VMEM((TILE, weight.shape[0]), jnp.bfloat16),
            pltpu.VMEM((cols,) + block, jnp.bfloat16),
            pltpu.VMEM((2,) + halves, jnp.bfloat16),
            pltpu.VMEM((nodes,) + halves, jnp.bfloat16),
            pltpu.VMEM((nodes, nodes + 1, 1, TILE), jnp.int32),
            pltpu.VMEM(block, jnp.int32),
            pltpu.VMEM(block, jnp.int32),
            pltpu.VMEM(block, jnp.bfloat16),
            pltpu.VMEM((nodes // 2, 2 * TILE, total), jnp.bfloat16),
            pltpu.VMEM((total, 2 * TILE), jnp.bfloat16),
            pltpu.VMEM((2,) + halves, jnp.bfloat16),
            pltpu.VMEM((nodes,) + halves, jnp.bfloat16),
            pltpu.VMEM((1, total), jnp.float32),
            pltpu.VMEM((TILE // 2, total), jnp.bfloat16),
            pltpu.VMEM((TILE // 2, total), jnp.float32),
            pltpu.VMEM((2, TILE // 2, total), jnp.bfloat16),
            pltpu.VMEM((2,) + halves, jnp.bfloat16),
            pltpu.VMEM((2,) + halves, jnp.bfloat16),
            pltpu.VMEM((2,) + halves, jnp.bfloat16),
            pltpu.VMEM((2 * cols,) + halves, jnp.bfloat16),
            pltpu.VMEM((nodes,) + halves, jnp.bfloat16),
            dma((7,)), dma((10,)), dma((13,)),
        ],
        compiler_params=pltpu.CompilerParams(collective_id=0, has_side_effects=True),
        name="layer",
    )(features, weight, degree[None, :], tile_cols, tile_count[None, :], tile_codes, cotangent)
    return pl.pallas_call(
        write_out_kernel,
        out_shape=tuple(jax.ShapeDtypeStruct(shape, dtype) for shape, dtype in outs),
        in_specs=[vmem] * 3,
        out_specs=(pl.BlockSpec(memory_space=pl.ANY),) * 3,
        scratch_shapes=[dma((3,))],
        name="write_out",
    )(*[pltpu.with_memory_space_constraint(x, pltpu.VMEM) for x in results])


def solution(mesh):
    in_specs = (
        P("nodes", "cols"),
        P(None, "cols"),
        P("nodes"),
        P("nodes", None),
        P("nodes"),
        P("nodes", None),
        P("nodes", "cols"),
    )
    out_specs = (P("nodes", "cols"), P(None, "cols"), P("nodes", "cols"))
    local = body
    shape = (mesh.shape["nodes"], mesh.shape["cols"])
    if shape == FUSED_SHAPE:
        local = functools.partial(fused, *shape)
    return jax.shard_map(local, mesh=mesh, in_specs=in_specs, out_specs=out_specs, check_vma=False)
```

```python
import functools

import jax
import jax.numpy as jnp
from jax import lax
from jax.experimental import pallas as pl
from jax.experimental.pallas import tpu as pltpu
from jax.sharding import PartitionSpec as P

MESH = pl.DeviceIdType.MESH

TILE = 128


def tile_bits(pattern_code):
    line_ids = jnp.arange(TILE, dtype=jnp.int32)
    hashed = (
        pattern_code[..., None, None] * 73856093
        ^ line_ids[:, None] * 19349663
        ^ line_ids[None, :] * 83492791
    )
    hashed = hashed ^ hashed >> 13
    hashed = hashed * 1274126177
    hashed = hashed ^ hashed >> 16
    return hashed & 63 == 0


def make_tiles(matches, code_table, live_limit, own, identity):
    slot_ids = jnp.arange(matches.shape[1], dtype=jnp.int32)
    slot_index = jnp.sum(jnp.where(matches, slot_ids[None, :], 0), axis=1, dtype=jnp.int32)
    code_value = jnp.sum(jnp.where(matches, code_table, 0), axis=1, dtype=jnp.int32)
    pattern = tile_bits(code_value) & (slot_index < live_limit)[:, None, None]
    values = (
        pattern.astype(jnp.float32)
        + jnp.where(own, 1.0, 0.0).astype(jnp.float32)[:, None, None] * identity
    )
    return values.astype(jnp.bfloat16)


def body(features, weight, degree, tile_cols, tile_count, tile_codes, cotangent):
    my_block = lax.axis_index("nodes")
    identity = jnp.eye(TILE, dtype=jnp.float32)
    inv_root = lax.rsqrt(degree.astype(jnp.float32))[:, None]
    scaled = (features.astype(jnp.float32) * inv_root).astype(jnp.bfloat16)
    my_cols = tile_cols[0]
    my_codes = tile_codes[0]
    my_count = tile_count[0]
    pieces = lax.all_gather(scaled[None], "nodes", axis=0, tiled=True)
    count_blocks = pieces.shape[0]
    targets = jnp.arange(count_blocks, dtype=jnp.int32)
    matches = targets[:, None] == my_cols[None, :]
    tiles = make_tiles(matches, my_codes[None, :], my_count, targets == my_block, identity)
    gathered = lax.dot_general(
        tiles, pieces, (((0, 2), (0, 1)), ((), ())), preferred_element_type=jnp.float32
    )
    aggregated = (inv_root * gathered).astype(jnp.bfloat16)
    agg_full = lax.all_gather(aggregated, "cols", axis=1, tiled=True)
    pre = jnp.dot(agg_full, weight, preferred_element_type=jnp.float32)
    activation = jax.nn.silu(pre).astype(jnp.bfloat16)
    sigma = jax.nn.sigmoid(pre)
    grad_pre = (cotangent.astype(jnp.float32) * sigma * (1.0 + pre * (1.0 - sigma))).astype(
        jnp.bfloat16
    )
    partial_grad = lax.dot_general(
        agg_full, grad_pre, (((0,), (0,)), ((), ())), preferred_element_type=jnp.float32
    )
    weight_grad = lax.psum(partial_grad, "nodes")
    terms = lax.dot_general(
        grad_pre, weight, (((1,), (1,)), ((), ())), preferred_element_type=jnp.float32
    )
    grad_agg = lax.psum_scatter(terms, "cols", scatter_dimension=1, tiled=True)
    grad_scaled = (inv_root * grad_agg).astype(jnp.bfloat16)
    all_cols, all_counts, all_codes = (
        lax.all_gather(tile_cols, "nodes", axis=0, tiled=True),
        lax.all_gather(tile_count, "nodes", axis=0, tiled=True),
        lax.all_gather(tile_codes, "nodes", axis=0, tiled=True),
    )
    pieces = lax.all_gather(grad_scaled[None], "nodes", axis=0, tiled=True)
    count_blocks = pieces.shape[0]
    row_ids = jnp.arange(count_blocks, dtype=jnp.int32)
    tiles = make_tiles(all_cols == my_block, all_codes, all_counts, row_ids == my_block, identity)
    back_total = lax.dot_general(
        tiles, pieces, (((0, 1), (0, 1)), ((), ())), preferred_element_type=jnp.float32
    )
    feats_grad = inv_root * back_total
    return (activation, weight_grad, feats_grad)


FUSED_SHAPE = (8, 4)

X, META, COT, W, Y, XT, U, WG, GRAD, ACT, Y_NEAR, Y_FAR = range(12)
SENDS = {META: 0, X: 1, COT: 1, W: 1, Y: 1, XT: 2, U: 2, GRAD: 2, WG: 3, ACT: 3}


def dot(a, b, dims):
    return lax.dot_general(a, b, (dims, ((), ())), preferred_element_type=jnp.float32)


def mul(a, b):
    return dot(a, b, ((1,), (0,)))


def turn(block):
    return jnp.transpose(block.astype(jnp.float32)).astype(jnp.bfloat16)


def hash_tile(code, base):
    hashed = (code * 73856093) ^ base
    hashed = hashed ^ hashed >> 13
    hashed = hashed * 1274126177
    hashed = hashed ^ hashed >> 16
    present = jnp.where(code >= 0, 1.0, 0.0)
    return jnp.where(hashed & 63 == 0, present, 0.0).astype(jnp.bfloat16)


def lanes(block):
    return pl.ds(pl.multiple_of(block * TILE, TILE), TILE)


def fused_kernel(
    nodes, cols,
    features_hbm, weight_hbm, degree_hbm, tile_cols_hbm, tile_count_hbm, tile_codes_hbm, cotangent_hbm,
    activation, weight_grad, feats_grad,
    features, weight, degree, tables, tile_count, cotangent,
    x_all, x_in, w_turned, w_all, cot_out, cot_in, meta, base, base_t, eye, adj_t, adj_own,
    y_out, y_in, d_row, agg, pre, grad, act_out, act_all, u_out, u_all, wg_all,
    load_sem, send_sem, recv_sem,
):
    n = lax.axis_index("nodes")
    c = lax.axis_index("cols")
    chips = nodes // 2
    chip, core = n // 2, lax.rem(n, 2)
    x_chip = chip + 1 - 2 * lax.rem(chip, 2)
    y_chip = lax.rem(chip + 2, chips)
    far_chip = lax.rem(x_chip + 2, chips)
    other = 1 - core
    partner = 2 * chip + other
    node_peers = [
        (2 * far_chip + core, core), (2 * far_chip + other, other),
        (2 * x_chip + core, core), (2 * x_chip + other, other),
        (2 * y_chip + core, core), (2 * y_chip + other, other),
        (partner, other),
    ]
    col_peers = [lax.rem(c + d, cols) for d in range(1, cols)]
    half = TILE // 2

    barrier = pltpu.get_barrier_semaphore()
    greeted = [(n, peer) for peer in col_peers] + [(partner, peer) for peer in col_peers]
    greeted += [(peer, c) for peer, _ in node_peers]
    for peer in greeted:
        pl.semaphore_signal(barrier, inc=1, device_id=peer, device_id_type=MESH)

    loads = []
    for i, (src, dst) in enumerate((
        (features_hbm, features), (tile_count_hbm, tile_count), (degree_hbm, degree),
        (tile_cols_hbm, tables.at[pl.ds(0, 1)]), (tile_codes_hbm, tables.at[pl.ds(1, 1)]),
        (cotangent_hbm, cotangent), (weight_hbm, weight),
    )):
        loads.append(pltpu.make_async_copy(src, dst, load_sem.at[(0, 1, 2, 3, 3, 4, 4)[i]]))
        loads[-1].start()

    def push(src, dst, peer, send, recv=None):
        pltpu.make_async_remote_copy(
            src_ref=src, dst_ref=dst, send_sem=send_sem.at[SENDS[send]], recv_sem=recv_sem.at[send if recv is None else recv],
            device_id=peer, device_id_type=MESH,
        ).start()

    def push_nodes(src_of, dst, send, far, near):
        recv = [far, far, send, send, send, send, near]
        for i, (peer, side) in enumerate(node_peers):
            push(src_of(peer, side), dst, (peer, c), send, recv[i])

    def wait_for(like, count, sem):
        whole = like if count == 0 else like.at[pl.ds(0, count)]
        pltpu.make_async_copy(whole, whole, sem).wait()

    def landed(like, count, recv):
        wait_for(like, count, recv_sem.at[recv])

    def left(tiles, send):
        wait_for(adj_t.at[0], tiles * (half * TILE // adj_t.shape[2]), send_sem.at[SENDS[send]])

    loads[0].wait()
    x_all[pl.ds(2 * c, 2)] = turn(features[...]).reshape(2, half, TILE)

    pl.semaphore_wait(barrier, len(greeted))

    orders = ((3, 2, 1), (2, 3, 0), (3, 0, 1), (0, 1, 2))
    x_order = [sum(jnp.where(c == at, order[i], 0) for at, order in enumerate(orders)) for i in range(cols - 1)]
    for peer in x_order:
        push(x_all.at[pl.ds(2 * c, 2)], x_all.at[pl.ds(2 * c, 2)], (n, peer), X)

    for load in loads[1:3]:
        load.wait()
    wait_for(tables, 0, load_sem.at[3])
    for block in range(nodes):
        code = jnp.int32(-1)
        for slot in range(nodes):
            hit = (tables[0, slot] == block) & (slot < tile_count[0, 0])
            code = jnp.where(hit, tables[1, slot], code)
        meta[n, block] = jnp.full((1, TILE), code, jnp.int32)
    meta[n, nodes] = degree[...]
    push_nodes(lambda peer, side: meta.at[n], meta.at[n], META, META, META)
    wait_for(adj_t.at[0], 10 * (half * TILE // adj_t.shape[2]), load_sem.at[4])
    cot_out[...] = turn(cotangent[...]).reshape(2, half, TILE)
    push_nodes(lambda peer, side: cot_out.at[side], cot_in.at[n], COT, COT, COT)
    cot_in[n] = cot_out[core]

    row_ids = lax.broadcasted_iota(jnp.int32, (TILE, TILE), 0)
    lane_ids = lax.broadcasted_iota(jnp.int32, (TILE, TILE), 1)
    eye[...] = jnp.where(row_ids == lane_ids, 1.0, 0.0).astype(jnp.bfloat16)
    base[...] = row_ids * 19349663 ^ lane_ids * 83492791
    base_t[...] = lane_ids * 19349663 ^ row_ids * 83492791
    for q in range(cols):
        w_turned[:, q * TILE:(q + 1) * TILE] = turn(weight[q * TILE:(q + 1) * TILE, :])
    w_all[c] = weight[lanes(c), :]

    def inv_row(row):
        return lax.rsqrt(meta[row, nodes].astype(jnp.float32))

    def make_row(row):
        d_row[:, lanes(row)] = inv_row(row)
        for block in range(nodes):
            at = (block % 2) * TILE
            adj_t[block // 2, at:at + TILE, lanes(row)] = hash_tile(meta[row, block], base_t[...])
        for side in range(2):
            at = side * TILE
            adj_own[lanes(row), at:at + TILE] = hash_tile(meta[row, 2 * chip + side], base[...])
        own = (row // 2, lanes(lax.rem(row, 2)), lanes(row))
        adj_t[own] = adj_t[own] + eye[...]

    make_row(n)
    landed(x_all, 2 * (cols - 1), X)
    y = mul(w_turned[...], x_all[...].reshape(cols * TILE, TILE)) * inv_row(n)
    y_out[...] = y.astype(jnp.bfloat16).reshape(2, half, TILE)
    push_nodes(lambda peer, side: y_out.at[side], y_in.at[n], Y, Y_FAR, Y_NEAR)
    push_nodes(lambda peer, side: x_all.at[peer], x_in.at[n], XT, XT, XT)
    for peer in col_peers:
        push(weight.at[lanes(peer), :], w_all.at[c], (n, peer), W)
    y_in[n] = y_out[core]
    x_in[n] = x_all[n]

    landed(meta, nodes - 1, META)
    make_row(partner)
    for side in range(2):
        own = (lanes(2 * chip + side), slice(side * TILE, (side + 1) * TILE))
        adj_own[own] = adj_own[own] + eye[...]

    def make_far(i, carry):
        make_row(lax.rem(2 * chip + i, nodes))
        return carry

    lax.fori_loop(2, nodes, make_far, 0)

    def chip_pair(buffer, at):
        return jnp.concatenate([buffer[2 * at], buffer[2 * at + 1]], axis=1)

    landed(cot_in, nodes - 1, COT)
    landed(y_in, 1, Y_NEAR)
    pre[...] = mul(chip_pair(y_in, chip), adj_t[chip])
    landed(y_in, 4, Y)
    pre[...] += mul(chip_pair(y_in, x_chip), adj_t[x_chip]) + mul(chip_pair(y_in, y_chip), adj_t[y_chip])
    landed(y_in, 2, Y_FAR)
    inv = d_row[...]
    value = (pre[...] + mul(chip_pair(y_in, far_chip), adj_t[far_chip])) * inv
    pre[...] = value
    sigma = 0.5 * jnp.tanh(0.5 * value) + 0.5
    cot = jnp.concatenate([cot_in[block] for block in range(nodes)], axis=1).astype(jnp.float32)
    grad[core] = (inv * (cot * sigma * (1.0 + value * (1.0 - sigma)))).astype(jnp.bfloat16)
    u = mul(grad[core], adj_own[...])
    for side in range(2):
        u_out[side] = (u[:, side * TILE:(side + 1) * TILE] * inv_row(2 * chip + side)).astype(jnp.bfloat16)
    here = u_all.at[2 * c + core]
    for peer in col_peers:
        push(u_out.at[core], here, (n, peer), U)
        push(u_out.at[other], here, (partner, peer), U)
    push(u_out.at[other], here, (partner, c), U)
    u_all[2 * c + core] = u_out[core]

    push(grad.at[core], grad.at[core], (partner, c), GRAD)
    for side, block in enumerate((n, partner)):
        own = pre[:, lanes(block)]
        act_out[side] = (own * jax.nn.sigmoid(own)).astype(jnp.bfloat16)
    push(act_out.at[1], act_all.at[core], (partner, c), ACT)
    act_all[core] = act_out[0]

    landed(x_in, nodes - 1, XT)
    scaled = jnp.concatenate([
        (x_in[block].astype(jnp.float32) * inv_row(block)).astype(jnp.bfloat16) for block in range(nodes)
    ], axis=1)
    for i in range(chips):
        part = slice(2 * i * TILE, 2 * (i + 1) * TILE)
        agg[:, part] = mul(scaled, adj_t[:, :, part].reshape(nodes * TILE, 2 * TILE)).astype(jnp.bfloat16)
    landed(grad, 1, GRAD)
    wg_all[n] = dot(agg[...], grad[...].reshape(TILE, nodes * TILE), ((1,), (1,))).astype(wg_all.dtype)
    push_nodes(lambda peer, side: wg_all.at[n], wg_all.at[n], WG, WG, WG)
    landed(act_all, 1, ACT)
    activation[...] = turn(act_all[...].reshape(TILE, TILE))

    wait_for(meta, nodes - 1, send_sem.at[SENDS[META]])
    left(4 * (cols - 1) + 2 * (nodes - 1), Y)
    left(nodes - 1 + 2 * cols - 1 + nodes, U)
    landed(w_all, cols - 1, W)
    landed(u_all, 2 * cols - 1, U)
    w_wide = jnp.concatenate([w_all[q] for q in range(cols)], axis=1)
    feats_grad[...] = jnp.transpose(mul(w_wide, u_all[...].reshape(cols * TILE, TILE)))

    landed(wg_all, nodes - 1, WG)
    for block in range(nodes):
        weight_grad[block * half:(block + 1) * half, :] = wg_all[block].astype(jnp.float32)
    left(nodes, WG)


def write_out_kernel(*refs):
    count = len(refs) // 2
    copies = [pltpu.make_async_copy(refs[i], refs[count + i], refs[-1].at[i]) for i in range(count)]
    for copy in copies:
        copy.start()
    for copy in copies:
        copy.wait()


def fused(nodes, cols, features, weight, degree, tile_cols, tile_count, tile_codes, cotangent):
    hbm = pl.BlockSpec(memory_space=pltpu.HBM)
    vmem = pl.BlockSpec(memory_space=pltpu.VMEM)
    block = (TILE, TILE)
    halves = (TILE // 2, TILE)
    total = nodes * TILE
    outs = ((features.shape, jnp.bfloat16), (weight.shape, jnp.float32), (features.shape, jnp.float32))
    dma = pltpu.SemaphoreType.DMA
    results = pl.pallas_call(
        functools.partial(fused_kernel, nodes, cols),
        out_shape=tuple(pltpu.VMEM(shape, dtype) for shape, dtype in outs),
        in_specs=[hbm] * 7,
        out_specs=(vmem, vmem, vmem),
        scratch_shapes=[
            pltpu.VMEM(features.shape, jnp.bfloat16),
            pltpu.VMEM(weight.shape, jnp.bfloat16),
            pltpu.VMEM((1, TILE), jnp.int32),
            pltpu.SMEM((2,) + tile_cols.shape[1:], jnp.int32),
            pltpu.SMEM((1, 1), jnp.int32),
            pltpu.VMEM(cotangent.shape, jnp.bfloat16),
            pltpu.VMEM((2 * cols,) + halves, jnp.bfloat16),
            pltpu.VMEM((nodes,) + halves, jnp.bfloat16),
            pltpu.VMEM((TILE, weight.shape[0]), jnp.bfloat16),
            pltpu.VMEM((cols,) + block, jnp.bfloat16),
            pltpu.VMEM((2,) + halves, jnp.bfloat16),
            pltpu.VMEM((nodes,) + halves, jnp.bfloat16),
            pltpu.VMEM((nodes, nodes + 1, 1, TILE), jnp.int32),
            pltpu.VMEM(block, jnp.int32),
            pltpu.VMEM(block, jnp.int32),
            pltpu.VMEM(block, jnp.bfloat16),
            pltpu.VMEM((nodes // 2, 2 * TILE, total), jnp.bfloat16),
            pltpu.VMEM((total, 2 * TILE), jnp.bfloat16),
            pltpu.VMEM((2,) + halves, jnp.bfloat16),
            pltpu.VMEM((nodes,) + halves, jnp.bfloat16),
            pltpu.VMEM((1, total), jnp.float32),
            pltpu.VMEM((TILE // 2, total), jnp.bfloat16),
            pltpu.VMEM((TILE // 2, total), jnp.float32),
            pltpu.VMEM((2, TILE // 2, total), jnp.bfloat16),
            pltpu.VMEM((2,) + halves, jnp.bfloat16),
            pltpu.VMEM((2,) + halves, jnp.bfloat16),
            pltpu.VMEM((2,) + halves, jnp.bfloat16),
            pltpu.VMEM((2 * cols,) + halves, jnp.bfloat16),
            pltpu.VMEM((nodes,) + halves, jnp.bfloat16),
            dma((5,)), dma((4,)), dma((12,)),
        ],
        compiler_params=pltpu.CompilerParams(collective_id=0, has_side_effects=True),
        name="layer",
    )(features, weight, degree[None, :], tile_cols, tile_count[None, :], tile_codes, cotangent)
    return pl.pallas_call(
        write_out_kernel,
        out_shape=tuple(jax.ShapeDtypeStruct(shape, dtype) for shape, dtype in outs),
        in_specs=[vmem] * 3,
        out_specs=(pl.BlockSpec(memory_space=pl.ANY),) * 3,
        scratch_shapes=[dma((3,))],
        name="write_out",
    )(*[pltpu.with_memory_space_constraint(x, pltpu.VMEM) for x in results])


def solution(mesh):
    in_specs = (
        P("nodes", "cols"),
        P(None, "cols"),
        P("nodes"),
        P("nodes", None),
        P("nodes"),
        P("nodes", None),
        P("nodes", "cols"),
    )
    out_specs = (P("nodes", "cols"), P(None, "cols"), P("nodes", "cols"))
    local = body
    shape = (mesh.shape["nodes"], mesh.shape["cols"])
    if shape == FUSED_SHAPE:
        local = functools.partial(fused, *shape)
    return jax.shard_map(local, mesh=mesh, in_specs=in_specs, out_specs=out_specs, check_vma=False)
```

```python
import functools

import jax
import jax.numpy as jnp
from jax import lax
from jax.experimental import pallas as pl
from jax.experimental.pallas import tpu as pltpu
from jax.sharding import PartitionSpec as P

MESH = pl.DeviceIdType.MESH

TILE = 128


def tile_bits(pattern_code):
    line_ids = jnp.arange(TILE, dtype=jnp.int32)
    hashed = (
        pattern_code[..., None, None] * 73856093
        ^ line_ids[:, None] * 19349663
        ^ line_ids[None, :] * 83492791
    )
    hashed = hashed ^ hashed >> 13
    hashed = hashed * 1274126177
    hashed = hashed ^ hashed >> 16
    return hashed & 63 == 0


def make_tiles(matches, code_table, live_limit, own, identity):
    slot_ids = jnp.arange(matches.shape[1], dtype=jnp.int32)
    slot_index = jnp.sum(jnp.where(matches, slot_ids[None, :], 0), axis=1, dtype=jnp.int32)
    code_value = jnp.sum(jnp.where(matches, code_table, 0), axis=1, dtype=jnp.int32)
    pattern = tile_bits(code_value) & (slot_index < live_limit)[:, None, None]
    values = (
        pattern.astype(jnp.float32)
        + jnp.where(own, 1.0, 0.0).astype(jnp.float32)[:, None, None] * identity
    )
    return values.astype(jnp.bfloat16)


def body(features, weight, degree, tile_cols, tile_count, tile_codes, cotangent):
    my_block = lax.axis_index("nodes")
    identity = jnp.eye(TILE, dtype=jnp.float32)
    inv_root = lax.rsqrt(degree.astype(jnp.float32))[:, None]
    scaled = (features.astype(jnp.float32) * inv_root).astype(jnp.bfloat16)
    my_cols = tile_cols[0]
    my_codes = tile_codes[0]
    my_count = tile_count[0]
    pieces = lax.all_gather(scaled[None], "nodes", axis=0, tiled=True)
    count_blocks = pieces.shape[0]
    targets = jnp.arange(count_blocks, dtype=jnp.int32)
    matches = targets[:, None] == my_cols[None, :]
    tiles = make_tiles(matches, my_codes[None, :], my_count, targets == my_block, identity)
    gathered = lax.dot_general(
        tiles, pieces, (((0, 2), (0, 1)), ((), ())), preferred_element_type=jnp.float32
    )
    aggregated = (inv_root * gathered).astype(jnp.bfloat16)
    agg_full = lax.all_gather(aggregated, "cols", axis=1, tiled=True)
    pre = jnp.dot(agg_full, weight, preferred_element_type=jnp.float32)
    activation = jax.nn.silu(pre).astype(jnp.bfloat16)
    sigma = jax.nn.sigmoid(pre)
    grad_pre = (cotangent.astype(jnp.float32) * sigma * (1.0 + pre * (1.0 - sigma))).astype(
        jnp.bfloat16
    )
    partial_grad = lax.dot_general(
        agg_full, grad_pre, (((0,), (0,)), ((), ())), preferred_element_type=jnp.float32
    )
    weight_grad = lax.psum(partial_grad, "nodes")
    terms = lax.dot_general(
        grad_pre, weight, (((1,), (1,)), ((), ())), preferred_element_type=jnp.float32
    )
    grad_agg = lax.psum_scatter(terms, "cols", scatter_dimension=1, tiled=True)
    grad_scaled = (inv_root * grad_agg).astype(jnp.bfloat16)
    all_cols, all_counts, all_codes = (
        lax.all_gather(tile_cols, "nodes", axis=0, tiled=True),
        lax.all_gather(tile_count, "nodes", axis=0, tiled=True),
        lax.all_gather(tile_codes, "nodes", axis=0, tiled=True),
    )
    pieces = lax.all_gather(grad_scaled[None], "nodes", axis=0, tiled=True)
    count_blocks = pieces.shape[0]
    row_ids = jnp.arange(count_blocks, dtype=jnp.int32)
    tiles = make_tiles(all_cols == my_block, all_codes, all_counts, row_ids == my_block, identity)
    back_total = lax.dot_general(
        tiles, pieces, (((0, 1), (0, 1)), ((), ())), preferred_element_type=jnp.float32
    )
    feats_grad = inv_root * back_total
    return (activation, weight_grad, feats_grad)


FUSED_SHAPE = (8, 4)

X, META, COT, W, Y, XT, U, WG, GRAD, ACT, Y_NEAR, Y_FAR = range(12)
SENDS = {META: 0, X: 1, COT: 1, W: 1, Y: 1, XT: 2, U: 2, GRAD: 2, WG: 3, ACT: 3}


def dot(a, b, dims):
    return lax.dot_general(a, b, (dims, ((), ())), preferred_element_type=jnp.float32)


def mul(a, b):
    return dot(a, b, ((1,), (0,)))


def turn(block):
    return jnp.transpose(block.astype(jnp.float32)).astype(jnp.bfloat16)


def hash_tile(code, base):
    hashed = (code * 73856093) ^ base
    hashed = hashed ^ hashed >> 13
    hashed = hashed * 1274126177
    hashed = hashed ^ hashed >> 16
    present = jnp.where(code >= 0, 1.0, 0.0)
    return jnp.where(hashed & 63 == 0, present, 0.0).astype(jnp.bfloat16)


def lanes(block):
    return pl.ds(pl.multiple_of(block * TILE, TILE), TILE)


def fused_kernel(
    nodes, cols,
    features_hbm, weight_hbm, degree_hbm, tile_cols_hbm, tile_count_hbm, tile_codes_hbm, cotangent_hbm,
    activation, weight_grad, feats_grad,
    features, weight, degree, tables, tile_count, cotangent,
    x_all, x_in, w_turned, w_all, cot_out, cot_in, meta, base, base_t, eye, adj_t, adj_own,
    y_out, y_in, d_row, agg, pre, grad, act_out, act_all, u_out, u_all, wg_all,
    load_sem, send_sem, recv_sem,
):
    n = lax.axis_index("nodes")
    c = lax.axis_index("cols")
    chips = nodes // 2
    chip, core = n // 2, lax.rem(n, 2)
    x_chip = chip + 1 - 2 * lax.rem(chip, 2)
    y_chip = lax.rem(chip + 2, chips)
    far_chip = lax.rem(x_chip + 2, chips)
    other = 1 - core
    partner = 2 * chip + other
    node_peers = [
        (2 * far_chip + core, core), (2 * far_chip + other, other),
        (2 * x_chip + core, core), (2 * x_chip + other, other),
        (2 * y_chip + core, core), (2 * y_chip + other, other),
        (partner, other),
    ]
    col_peers = [lax.rem(c + d, cols) for d in range(1, cols)]
    half = TILE // 2

    barrier = pltpu.get_barrier_semaphore()
    greeted = [(n, peer) for peer in col_peers] + [(partner, peer) for peer in col_peers]
    greeted += [(peer, c) for peer, _ in node_peers]
    for peer in greeted:
        pl.semaphore_signal(barrier, inc=1, device_id=peer, device_id_type=MESH)

    loads = []
    for i, (src, dst) in enumerate((
        (features_hbm, features), (tile_count_hbm, tile_count), (degree_hbm, degree),
        (tile_cols_hbm, tables.at[pl.ds(0, 1)]), (tile_codes_hbm, tables.at[pl.ds(1, 1)]),
        (cotangent_hbm, cotangent), (weight_hbm, weight),
    )):
        loads.append(pltpu.make_async_copy(src, dst, load_sem.at[(0, 1, 2, 3, 3, 4, 4)[i]]))
        loads[-1].start()

    def push(src, dst, peer, send, recv=None):
        pltpu.make_async_remote_copy(
            src_ref=src, dst_ref=dst, send_sem=send_sem.at[SENDS[send]], recv_sem=recv_sem.at[send if recv is None else recv],
            device_id=peer, device_id_type=MESH,
        ).start()

    def push_nodes(src_of, dst, send, far, near):
        recv = [far, far, send, send, send, send, near]
        for i, (peer, side) in enumerate(node_peers):
            push(src_of(peer, side), dst, (peer, c), send, recv[i])

    def wait_for(like, count, sem):
        whole = like if count == 0 else like.at[pl.ds(0, count)]
        pltpu.make_async_copy(whole, whole, sem).wait()

    def landed(like, count, recv):
        wait_for(like, count, recv_sem.at[recv])

    def left(tiles, send):
        wait_for(adj_t.at[0], tiles * (half * TILE // adj_t.shape[2]), send_sem.at[SENDS[send]])

    loads[0].wait()
    x_all[pl.ds(2 * c, 2)] = turn(features[...]).reshape(2, half, TILE)

    pl.semaphore_wait(barrier, len(greeted))

    orders = ((3, 2, 1), (2, 3, 0), (3, 0, 1), (0, 1, 2))
    x_order = [sum(jnp.where(c == at, order[i], 0) for at, order in enumerate(orders)) for i in range(cols - 1)]
    for peer in x_order:
        push(x_all.at[pl.ds(2 * c, 2)], x_all.at[pl.ds(2 * c, 2)], (n, peer), X)

    for load in loads[1:3]:
        load.wait()
    wait_for(tables, 0, load_sem.at[3])
    for block in range(nodes):
        code = jnp.int32(-1)
        for slot in range(nodes):
            hit = (tables[0, slot] == block) & (slot < tile_count[0, 0])
            code = jnp.where(hit, tables[1, slot], code)
        meta[n, block] = jnp.full((1, TILE), code, jnp.int32)
    meta[n, nodes] = degree[...]
    push_nodes(lambda peer, side: meta.at[n], meta.at[n], META, META, META)
    wait_for(adj_t.at[0], 10 * (half * TILE // adj_t.shape[2]), load_sem.at[4])
    cot_out[...] = turn(cotangent[...]).reshape(2, half, TILE)
    push_nodes(lambda peer, side: cot_out.at[side], cot_in.at[n], COT, COT, COT)
    cot_in[n] = cot_out[core]

    row_ids = lax.broadcasted_iota(jnp.int32, (TILE, TILE), 0)
    lane_ids = lax.broadcasted_iota(jnp.int32, (TILE, TILE), 1)
    eye[...] = jnp.where(row_ids == lane_ids, 1.0, 0.0).astype(jnp.bfloat16)
    base[...] = row_ids * 19349663 ^ lane_ids * 83492791
    base_t[...] = lane_ids * 19349663 ^ row_ids * 83492791
    for q in range(cols):
        w_turned[:, q * TILE:(q + 1) * TILE] = turn(weight[q * TILE:(q + 1) * TILE, :])
    w_all[c] = weight[lanes(c), :]

    def inv_row(row):
        return lax.rsqrt(meta[row, nodes].astype(jnp.float32))

    def make_row(row):
        d_row[:, lanes(row)] = inv_row(row)
        for block in range(nodes):
            at = (block % 2) * TILE
            adj_t[block // 2, at:at + TILE, lanes(row)] = hash_tile(meta[row, block], base_t[...])
        for side in range(2):
            at = side * TILE
            adj_own[lanes(row), at:at + TILE] = hash_tile(meta[row, 2 * chip + side], base[...])
        own = (row // 2, lanes(lax.rem(row, 2)), lanes(row))
        adj_t[own] = adj_t[own] + eye[...]

    make_row(n)
    landed(x_all, 2 * (cols - 1), X)
    y = mul(w_turned[...], x_all[...].reshape(cols * TILE, TILE)) * inv_row(n)
    y_out[...] = y.astype(jnp.bfloat16).reshape(2, half, TILE)
    push_nodes(lambda peer, side: y_out.at[side], y_in.at[n], Y, Y_FAR, Y_NEAR)
    push_nodes(lambda peer, side: x_all.at[peer], x_in.at[n], XT, XT, XT)
    for peer in col_peers:
        push(weight.at[lanes(peer), :], w_all.at[c], (n, peer), W)
    y_in[n] = y_out[core]
    x_in[n] = x_all[n]

    landed(meta, nodes - 1, META)
    make_row(partner)
    for side in range(2):
        own = (lanes(2 * chip + side), slice(side * TILE, (side + 1) * TILE))
        adj_own[own] = adj_own[own] + eye[...]

    def make_far(i, carry):
        make_row(lax.rem(2 * chip + i, nodes))
        return carry

    lax.fori_loop(2, nodes, make_far, 0)

    def chip_pair(buffer, at):
        return jnp.concatenate([buffer[2 * at], buffer[2 * at + 1]], axis=1)

    landed(cot_in, nodes - 1, COT)
    landed(y_in, 1, Y_NEAR)
    pre[...] = mul(chip_pair(y_in, chip), adj_t[chip])
    landed(y_in, 4, Y)
    pre[...] += mul(chip_pair(y_in, x_chip), adj_t[x_chip]) + mul(chip_pair(y_in, y_chip), adj_t[y_chip])
    landed(y_in, 2, Y_FAR)
    inv = d_row[...]
    value = (pre[...] + mul(chip_pair(y_in, far_chip), adj_t[far_chip])) * inv
    pre[...] = value
    sigma = 0.5 * jnp.tanh(0.5 * value) + 0.5
    cot = jnp.concatenate([cot_in[block] for block in range(nodes)], axis=1).astype(jnp.float32)
    grad[core] = (inv * (cot * sigma * (1.0 + value * (1.0 - sigma)))).astype(jnp.bfloat16)
    push(grad.at[core], grad.at[core], (partner, c), GRAD)
    u = mul(grad[core], adj_own[...])
    for side in range(2):
        u_out[side] = (u[:, side * TILE:(side + 1) * TILE] * inv_row(2 * chip + side)).astype(jnp.bfloat16)
    here = u_all.at[2 * c + core]
    for peer in col_peers:
        push(u_out.at[core], here, (n, peer), U)
        push(u_out.at[other], here, (partner, peer), U)
    push(u_out.at[other], here, (partner, c), U)
    u_all[2 * c + core] = u_out[core]

    landed(x_in, nodes - 1, XT)
    scaled = jnp.concatenate([
        (x_in[block].astype(jnp.float32) * inv_row(block)).astype(jnp.bfloat16) for block in range(nodes)
    ], axis=1)
    for i in range(chips):
        part = slice(2 * i * TILE, 2 * (i + 1) * TILE)
        agg[:, part] = mul(scaled, adj_t[:, :, part].reshape(nodes * TILE, 2 * TILE)).astype(jnp.bfloat16)
    landed(grad, 1, GRAD)
    wg_all[n] = dot(agg[...], grad[...].reshape(TILE, nodes * TILE), ((1,), (1,))).astype(wg_all.dtype)
    push_nodes(lambda peer, side: wg_all.at[n], wg_all.at[n], WG, WG, WG)
    for side, block in enumerate((n, partner)):
        own = pre[:, lanes(block)]
        act_out[side] = (own * jax.nn.sigmoid(own)).astype(jnp.bfloat16)
    push(act_out.at[1], act_all.at[core], (partner, c), ACT)
    act_all[core] = act_out[0]

    landed(act_all, 1, ACT)
    activation[...] = turn(act_all[...].reshape(TILE, TILE))

    wait_for(meta, nodes - 1, send_sem.at[SENDS[META]])
    left(4 * (cols - 1) + 2 * (nodes - 1), Y)
    left(nodes - 1 + 2 * cols - 1 + nodes, U)
    landed(w_all, cols - 1, W)
    landed(u_all, 2 * cols - 1, U)
    w_wide = jnp.concatenate([w_all[q] for q in range(cols)], axis=1)
    feats_grad[...] = jnp.transpose(mul(w_wide, u_all[...].reshape(cols * TILE, TILE)))

    landed(wg_all, nodes - 1, WG)
    for block in range(nodes):
        weight_grad[block * half:(block + 1) * half, :] = wg_all[block].astype(jnp.float32)
    left(nodes, WG)


def write_out_kernel(*refs):
    count = len(refs) // 2
    copies = [pltpu.make_async_copy(refs[i], refs[count + i], refs[-1].at[i]) for i in range(count)]
    for copy in copies:
        copy.start()
    for copy in copies:
        copy.wait()


def fused(nodes, cols, features, weight, degree, tile_cols, tile_count, tile_codes, cotangent):
    hbm = pl.BlockSpec(memory_space=pltpu.HBM)
    vmem = pl.BlockSpec(memory_space=pltpu.VMEM)
    block = (TILE, TILE)
    halves = (TILE // 2, TILE)
    total = nodes * TILE
    outs = ((features.shape, jnp.bfloat16), (weight.shape, jnp.float32), (features.shape, jnp.float32))
    dma = pltpu.SemaphoreType.DMA
    results = pl.pallas_call(
        functools.partial(fused_kernel, nodes, cols),
        out_shape=tuple(pltpu.VMEM(shape, dtype) for shape, dtype in outs),
        in_specs=[hbm] * 7,
        out_specs=(vmem, vmem, vmem),
        scratch_shapes=[
            pltpu.VMEM(features.shape, jnp.bfloat16),
            pltpu.VMEM(weight.shape, jnp.bfloat16),
            pltpu.VMEM((1, TILE), jnp.int32),
            pltpu.SMEM((2,) + tile_cols.shape[1:], jnp.int32),
            pltpu.SMEM((1, 1), jnp.int32),
            pltpu.VMEM(cotangent.shape, jnp.bfloat16),
            pltpu.VMEM((2 * cols,) + halves, jnp.bfloat16),
            pltpu.VMEM((nodes,) + halves, jnp.bfloat16),
            pltpu.VMEM((TILE, weight.shape[0]), jnp.bfloat16),
            pltpu.VMEM((cols,) + block, jnp.bfloat16),
            pltpu.VMEM((2,) + halves, jnp.bfloat16),
            pltpu.VMEM((nodes,) + halves, jnp.bfloat16),
            pltpu.VMEM((nodes, nodes + 1, 1, TILE), jnp.int32),
            pltpu.VMEM(block, jnp.int32),
            pltpu.VMEM(block, jnp.int32),
            pltpu.VMEM(block, jnp.bfloat16),
            pltpu.VMEM((nodes // 2, 2 * TILE, total), jnp.bfloat16),
            pltpu.VMEM((total, 2 * TILE), jnp.bfloat16),
            pltpu.VMEM((2,) + halves, jnp.bfloat16),
            pltpu.VMEM((nodes,) + halves, jnp.bfloat16),
            pltpu.VMEM((1, total), jnp.float32),
            pltpu.VMEM((TILE // 2, total), jnp.bfloat16),
            pltpu.VMEM((TILE // 2, total), jnp.float32),
            pltpu.VMEM((2, TILE // 2, total), jnp.bfloat16),
            pltpu.VMEM((2,) + halves, jnp.bfloat16),
            pltpu.VMEM((2,) + halves, jnp.bfloat16),
            pltpu.VMEM((2,) + halves, jnp.bfloat16),
            pltpu.VMEM((2 * cols,) + halves, jnp.bfloat16),
            pltpu.VMEM((nodes,) + halves, jnp.bfloat16),
            dma((5,)), dma((4,)), dma((12,)),
        ],
        compiler_params=pltpu.CompilerParams(collective_id=0, has_side_effects=True),
        name="layer",
    )(features, weight, degree[None, :], tile_cols, tile_count[None, :], tile_codes, cotangent)
    return pl.pallas_call(
        write_out_kernel,
        out_shape=tuple(jax.ShapeDtypeStruct(shape, dtype) for shape, dtype in outs),
        in_specs=[vmem] * 3,
        out_specs=(pl.BlockSpec(memory_space=pl.ANY),) * 3,
        scratch_shapes=[dma((3,))],
        name="write_out",
    )(*[pltpu.with_memory_space_constraint(x, pltpu.VMEM) for x in results])


def solution(mesh):
    in_specs = (
        P("nodes", "cols"),
        P(None, "cols"),
        P("nodes"),
        P("nodes", None),
        P("nodes"),
        P("nodes", None),
        P("nodes", "cols"),
    )
    out_specs = (P("nodes", "cols"), P(None, "cols"), P("nodes", "cols"))
    local = body
    shape = (mesh.shape["nodes"], mesh.shape["cols"])
    if shape == FUSED_SHAPE:
        local = functools.partial(fused, *shape)
    return jax.shard_map(local, mesh=mesh, in_specs=in_specs, out_specs=out_specs, check_vma=False)
```

```python
import functools

import jax
import jax.numpy as jnp
from jax import lax
from jax.experimental import pallas as pl
from jax.experimental.pallas import tpu as pltpu
from jax.sharding import PartitionSpec as P

MESH = pl.DeviceIdType.MESH

TILE = 128


def tile_bits(pattern_code):
    line_ids = jnp.arange(TILE, dtype=jnp.int32)
    hashed = (
        pattern_code[..., None, None] * 73856093
        ^ line_ids[:, None] * 19349663
        ^ line_ids[None, :] * 83492791
    )
    hashed = hashed ^ hashed >> 13
    hashed = hashed * 1274126177
    hashed = hashed ^ hashed >> 16
    return hashed & 63 == 0


def make_tiles(matches, code_table, live_limit, own, identity):
    slot_ids = jnp.arange(matches.shape[1], dtype=jnp.int32)
    slot_index = jnp.sum(jnp.where(matches, slot_ids[None, :], 0), axis=1, dtype=jnp.int32)
    code_value = jnp.sum(jnp.where(matches, code_table, 0), axis=1, dtype=jnp.int32)
    pattern = tile_bits(code_value) & (slot_index < live_limit)[:, None, None]
    values = (
        pattern.astype(jnp.float32)
        + jnp.where(own, 1.0, 0.0).astype(jnp.float32)[:, None, None] * identity
    )
    return values.astype(jnp.bfloat16)


def body(features, weight, degree, tile_cols, tile_count, tile_codes, cotangent):
    my_block = lax.axis_index("nodes")
    identity = jnp.eye(TILE, dtype=jnp.float32)
    inv_root = lax.rsqrt(degree.astype(jnp.float32))[:, None]
    scaled = (features.astype(jnp.float32) * inv_root).astype(jnp.bfloat16)
    my_cols = tile_cols[0]
    my_codes = tile_codes[0]
    my_count = tile_count[0]
    pieces = lax.all_gather(scaled[None], "nodes", axis=0, tiled=True)
    count_blocks = pieces.shape[0]
    targets = jnp.arange(count_blocks, dtype=jnp.int32)
    matches = targets[:, None] == my_cols[None, :]
    tiles = make_tiles(matches, my_codes[None, :], my_count, targets == my_block, identity)
    gathered = lax.dot_general(
        tiles, pieces, (((0, 2), (0, 1)), ((), ())), preferred_element_type=jnp.float32
    )
    aggregated = (inv_root * gathered).astype(jnp.bfloat16)
    agg_full = lax.all_gather(aggregated, "cols", axis=1, tiled=True)
    pre = jnp.dot(agg_full, weight, preferred_element_type=jnp.float32)
    activation = jax.nn.silu(pre).astype(jnp.bfloat16)
    sigma = jax.nn.sigmoid(pre)
    grad_pre = (cotangent.astype(jnp.float32) * sigma * (1.0 + pre * (1.0 - sigma))).astype(
        jnp.bfloat16
    )
    partial_grad = lax.dot_general(
        agg_full, grad_pre, (((0,), (0,)), ((), ())), preferred_element_type=jnp.float32
    )
    weight_grad = lax.psum(partial_grad, "nodes")
    terms = lax.dot_general(
        grad_pre, weight, (((1,), (1,)), ((), ())), preferred_element_type=jnp.float32
    )
    grad_agg = lax.psum_scatter(terms, "cols", scatter_dimension=1, tiled=True)
    grad_scaled = (inv_root * grad_agg).astype(jnp.bfloat16)
    all_cols, all_counts, all_codes = (
        lax.all_gather(tile_cols, "nodes", axis=0, tiled=True),
        lax.all_gather(tile_count, "nodes", axis=0, tiled=True),
        lax.all_gather(tile_codes, "nodes", axis=0, tiled=True),
    )
    pieces = lax.all_gather(grad_scaled[None], "nodes", axis=0, tiled=True)
    count_blocks = pieces.shape[0]
    row_ids = jnp.arange(count_blocks, dtype=jnp.int32)
    tiles = make_tiles(all_cols == my_block, all_codes, all_counts, row_ids == my_block, identity)
    back_total = lax.dot_general(
        tiles, pieces, (((0, 1), (0, 1)), ((), ())), preferred_element_type=jnp.float32
    )
    feats_grad = inv_root * back_total
    return (activation, weight_grad, feats_grad)


FUSED_SHAPE = (8, 4)

X, META, COT, W, Y, XT, U, WG, GRAD, ACT, Y_NEAR, Y_FAR = range(12)
SENDS = {META: 0, X: 1, COT: 1, W: 1, Y: 1, XT: 2, U: 2, GRAD: 2, WG: 3, ACT: 3}


def dot(a, b, dims):
    return lax.dot_general(a, b, (dims, ((), ())), preferred_element_type=jnp.float32)


def mul(a, b):
    return dot(a, b, ((1,), (0,)))


def turn(block):
    return jnp.transpose(block.astype(jnp.float32)).astype(jnp.bfloat16)


def hash_tile(code, base):
    hashed = (code * 73856093) ^ base
    hashed = hashed ^ hashed >> 13
    hashed = hashed * 1274126177
    hashed = hashed ^ hashed >> 16
    present = jnp.where(code >= 0, 1.0, 0.0)
    return jnp.where(hashed & 63 == 0, present, 0.0).astype(jnp.bfloat16)


def lanes(block):
    return pl.ds(pl.multiple_of(block * TILE, TILE), TILE)


def fused_kernel(
    nodes, cols,
    features_hbm, weight_hbm, degree_hbm, tile_cols_hbm, tile_count_hbm, tile_codes_hbm, cotangent_hbm,
    activation, weight_grad, feats_grad,
    features, weight, degree, tables, tile_count, cotangent,
    x_all, x_in, w_turned, w_all, cot_out, cot_in, meta, base, base_t, eye, adj_t, adj_own,
    y_out, y_in, d_row, agg, pre, grad, act_out, act_all, u_out, u_all, wg_all,
    load_sem, send_sem, recv_sem,
):
    n = lax.axis_index("nodes")
    c = lax.axis_index("cols")
    chips = nodes // 2
    chip, core = n // 2, lax.rem(n, 2)
    x_chip = chip + 1 - 2 * lax.rem(chip, 2)
    y_chip = lax.rem(chip + 2, chips)
    far_chip = lax.rem(x_chip + 2, chips)
    other = 1 - core
    partner = 2 * chip + other
    node_peers = [
        (2 * far_chip + core, core), (2 * far_chip + other, other),
        (2 * x_chip + core, core), (2 * x_chip + other, other),
        (2 * y_chip + core, core), (2 * y_chip + other, other),
        (partner, other),
    ]
    col_peers = [lax.rem(c + d, cols) for d in range(1, cols)]
    half = TILE // 2

    barrier = pltpu.get_barrier_semaphore()
    greeted = [(n, peer) for peer in col_peers] + [(partner, peer) for peer in col_peers]
    greeted += [(peer, c) for peer, _ in node_peers]
    for peer in greeted:
        pl.semaphore_signal(barrier, inc=1, device_id=peer, device_id_type=MESH)

    loads = []
    for i, (src, dst) in enumerate((
        (features_hbm, features), (tile_count_hbm, tile_count), (degree_hbm, degree),
        (tile_cols_hbm, tables.at[pl.ds(0, 1)]), (tile_codes_hbm, tables.at[pl.ds(1, 1)]),
        (cotangent_hbm, cotangent), (weight_hbm, weight),
    )):
        loads.append(pltpu.make_async_copy(src, dst, load_sem.at[(0, 1, 2, 3, 3, 4, 4)[i]]))
        loads[-1].start()

    def push(src, dst, peer, send, recv=None):
        pltpu.make_async_remote_copy(
            src_ref=src, dst_ref=dst, send_sem=send_sem.at[SENDS[send]], recv_sem=recv_sem.at[send if recv is None else recv],
            device_id=peer, device_id_type=MESH,
        ).start()

    def push_nodes(src_of, dst, send, far, near):
        recv = [far, far, send, send, send, send, near]
        for i, (peer, side) in enumerate(node_peers):
            push(src_of(peer, side), dst, (peer, c), send, recv[i])

    def wait_for(like, count, sem):
        whole = like if count == 0 else like.at[pl.ds(0, count)]
        pltpu.make_async_copy(whole, whole, sem).wait()

    def landed(like, count, recv):
        wait_for(like, count, recv_sem.at[recv])

    def left(tiles, send):
        wait_for(adj_t.at[0], tiles * (half * TILE // adj_t.shape[2]), send_sem.at[SENDS[send]])

    loads[0].wait()
    x_all[pl.ds(2 * c, 2)] = turn(features[...]).reshape(2, half, TILE)

    pl.semaphore_wait(barrier, len(greeted))

    orders = ((3, 2, 1), (2, 3, 0), (3, 0, 1), (0, 1, 2))
    x_order = [sum(jnp.where(c == at, order[i], 0) for at, order in enumerate(orders)) for i in range(cols - 1)]
    for peer in x_order:
        push(x_all.at[pl.ds(2 * c, 2)], x_all.at[pl.ds(2 * c, 2)], (n, peer), X)

    for load in loads[1:3]:
        load.wait()
    wait_for(tables, 0, load_sem.at[3])
    for block in range(nodes):
        code = jnp.int32(-1)
        for slot in range(nodes):
            hit = (tables[0, slot] == block) & (slot < tile_count[0, 0])
            code = jnp.where(hit, tables[1, slot], code)
        meta[n, block] = jnp.full((1, TILE), code, jnp.int32)
    meta[n, nodes] = degree[...]
    push_nodes(lambda peer, side: meta.at[n], meta.at[n], META, META, META)
    wait_for(adj_t.at[0], 10 * (half * TILE // adj_t.shape[2]), load_sem.at[4])
    cot_out[...] = turn(cotangent[...]).reshape(2, half, TILE)
    push_nodes(lambda peer, side: cot_out.at[side], cot_in.at[n], COT, COT, COT)
    cot_in[n] = cot_out[core]

    row_ids = lax.broadcasted_iota(jnp.int32, (TILE, TILE), 0)
    lane_ids = lax.broadcasted_iota(jnp.int32, (TILE, TILE), 1)
    eye[...] = jnp.where(row_ids == lane_ids, 1.0, 0.0).astype(jnp.bfloat16)
    base[...] = row_ids * 19349663 ^ lane_ids * 83492791
    base_t[...] = lane_ids * 19349663 ^ row_ids * 83492791
    for q in range(cols):
        w_turned[:, q * TILE:(q + 1) * TILE] = turn(weight[q * TILE:(q + 1) * TILE, :])
    w_all[c] = weight[lanes(c), :]

    def inv_row(row):
        return lax.rsqrt(meta[row, nodes].astype(jnp.float32))

    def make_row(row):
        d_row[:, lanes(row)] = inv_row(row)
        for block in range(nodes):
            at = (block % 2) * TILE
            adj_t[block // 2, at:at + TILE, lanes(row)] = hash_tile(meta[row, block], base_t[...])
        for side in range(2):
            at = side * TILE
            adj_own[lanes(row), at:at + TILE] = hash_tile(meta[row, 2 * chip + side], base[...])
        own = (row // 2, lanes(lax.rem(row, 2)), lanes(row))
        adj_t[own] = adj_t[own] + eye[...]

    make_row(n)
    landed(x_all, 2 * (cols - 1), X)
    y = mul(w_turned[...], x_all[...].reshape(cols * TILE, TILE)) * inv_row(n)
    y_out[...] = y.astype(jnp.bfloat16).reshape(2, half, TILE)
    push_nodes(lambda peer, side: y_out.at[side], y_in.at[n], Y, Y_FAR, Y_NEAR)
    push_nodes(lambda peer, side: x_all.at[peer], x_in.at[n], XT, XT, XT)
    for peer in col_peers:
        push(weight.at[lanes(peer), :], w_all.at[c], (n, peer), W)
    y_in[n] = y_out[core]
    x_in[n] = x_all[n]

    landed(meta, nodes - 1, META)
    make_row(partner)
    for side in range(2):
        own = (lanes(2 * chip + side), slice(side * TILE, (side + 1) * TILE))
        adj_own[own] = adj_own[own] + eye[...]

    def make_far(i, carry):
        make_row(lax.rem(2 * chip + i, nodes))
        return carry

    lax.fori_loop(2, nodes, make_far, 0)

    def chip_pair(buffer, at):
        return jnp.concatenate([buffer[2 * at], buffer[2 * at + 1]], axis=1)

    landed(cot_in, nodes - 1, COT)
    landed(y_in, 1, Y_NEAR)
    pre[...] = mul(chip_pair(y_in, chip), adj_t[chip])
    landed(y_in, 4, Y)
    pre[...] += mul(chip_pair(y_in, x_chip), adj_t[x_chip]) + mul(chip_pair(y_in, y_chip), adj_t[y_chip])
    landed(y_in, 2, Y_FAR)
    inv = d_row[...]
    value = (pre[...] + mul(chip_pair(y_in, far_chip), adj_t[far_chip])) * inv
    pre[...] = value
    sigma = 0.5 * jnp.tanh(0.5 * value) + 0.5
    cot = jnp.concatenate([cot_in[block] for block in range(nodes)], axis=1).astype(jnp.float32)
    grad[core] = (inv * (cot * sigma * (1.0 + value * (1.0 - sigma)))).astype(jnp.bfloat16)
    push(grad.at[core], grad.at[core], (partner, c), GRAD)
    u = mul(grad[core], adj_own[...])
    for side in range(2):
        u_out[side] = (u[:, side * TILE:(side + 1) * TILE] * inv_row(2 * chip + side)).astype(jnp.bfloat16)
    here = u_all.at[2 * c + core]
    for peer in x_order:
        push(u_out.at[core], here, (n, peer), U)
        push(u_out.at[other], here, (partner, peer), U)
    push(u_out.at[other], here, (partner, c), U)
    u_all[2 * c + core] = u_out[core]

    landed(x_in, nodes - 1, XT)
    scaled = jnp.concatenate([
        (x_in[block].astype(jnp.float32) * inv_row(block)).astype(jnp.bfloat16) for block in range(nodes)
    ], axis=1)
    for i in range(chips):
        part = slice(2 * i * TILE, 2 * (i + 1) * TILE)
        agg[:, part] = mul(scaled, adj_t[:, :, part].reshape(nodes * TILE, 2 * TILE)).astype(jnp.bfloat16)
    landed(grad, 1, GRAD)
    wg_all[n] = dot(agg[...], grad[...].reshape(TILE, nodes * TILE), ((1,), (1,))).astype(wg_all.dtype)
    push_nodes(lambda peer, side: wg_all.at[n], wg_all.at[n], WG, WG, WG)
    for side, block in enumerate((n, partner)):
        own = pre[:, lanes(block)]
        act_out[side] = (own * jax.nn.sigmoid(own)).astype(jnp.bfloat16)
    push(act_out.at[1], act_all.at[core], (partner, c), ACT)
    act_all[core] = act_out[0]

    landed(act_all, 1, ACT)
    activation[...] = turn(act_all[...].reshape(TILE, TILE))

    wait_for(meta, nodes - 1, send_sem.at[SENDS[META]])
    left(4 * (cols - 1) + 2 * (nodes - 1), Y)
    left(nodes - 1 + 2 * cols - 1 + nodes, U)
    landed(w_all, cols - 1, W)
    landed(u_all, 2 * cols - 1, U)
    w_wide = jnp.concatenate([w_all[q] for q in range(cols)], axis=1)
    feats_grad[...] = jnp.transpose(mul(w_wide, u_all[...].reshape(cols * TILE, TILE)))

    landed(wg_all, nodes - 1, WG)
    for block in range(nodes):
        weight_grad[block * half:(block + 1) * half, :] = wg_all[block].astype(jnp.float32)
    left(nodes, WG)


def write_out_kernel(*refs):
    count = len(refs) // 2
    copies = [pltpu.make_async_copy(refs[i], refs[count + i], refs[-1].at[i]) for i in range(count)]
    for copy in copies:
        copy.start()
    for copy in copies:
        copy.wait()


def fused(nodes, cols, features, weight, degree, tile_cols, tile_count, tile_codes, cotangent):
    hbm = pl.BlockSpec(memory_space=pltpu.HBM)
    vmem = pl.BlockSpec(memory_space=pltpu.VMEM)
    block = (TILE, TILE)
    halves = (TILE // 2, TILE)
    total = nodes * TILE
    outs = ((features.shape, jnp.bfloat16), (weight.shape, jnp.float32), (features.shape, jnp.float32))
    dma = pltpu.SemaphoreType.DMA
    results = pl.pallas_call(
        functools.partial(fused_kernel, nodes, cols),
        out_shape=tuple(pltpu.VMEM(shape, dtype) for shape, dtype in outs),
        in_specs=[hbm] * 7,
        out_specs=(vmem, vmem, vmem),
        scratch_shapes=[
            pltpu.VMEM(features.shape, jnp.bfloat16),
            pltpu.VMEM(weight.shape, jnp.bfloat16),
            pltpu.VMEM((1, TILE), jnp.int32),
            pltpu.SMEM((2,) + tile_cols.shape[1:], jnp.int32),
            pltpu.SMEM((1, 1), jnp.int32),
            pltpu.VMEM(cotangent.shape, jnp.bfloat16),
            pltpu.VMEM((2 * cols,) + halves, jnp.bfloat16),
            pltpu.VMEM((nodes,) + halves, jnp.bfloat16),
            pltpu.VMEM((TILE, weight.shape[0]), jnp.bfloat16),
            pltpu.VMEM((cols,) + block, jnp.bfloat16),
            pltpu.VMEM((2,) + halves, jnp.bfloat16),
            pltpu.VMEM((nodes,) + halves, jnp.bfloat16),
            pltpu.VMEM((nodes, nodes + 1, 1, TILE), jnp.int32),
            pltpu.VMEM(block, jnp.int32),
            pltpu.VMEM(block, jnp.int32),
            pltpu.VMEM(block, jnp.bfloat16),
            pltpu.VMEM((nodes // 2, 2 * TILE, total), jnp.bfloat16),
            pltpu.VMEM((total, 2 * TILE), jnp.bfloat16),
            pltpu.VMEM((2,) + halves, jnp.bfloat16),
            pltpu.VMEM((nodes,) + halves, jnp.bfloat16),
            pltpu.VMEM((1, total), jnp.float32),
            pltpu.VMEM((TILE // 2, total), jnp.bfloat16),
            pltpu.VMEM((TILE // 2, total), jnp.float32),
            pltpu.VMEM((2, TILE // 2, total), jnp.bfloat16),
            pltpu.VMEM((2,) + halves, jnp.bfloat16),
            pltpu.VMEM((2,) + halves, jnp.bfloat16),
            pltpu.VMEM((2,) + halves, jnp.bfloat16),
            pltpu.VMEM((2 * cols,) + halves, jnp.bfloat16),
            pltpu.VMEM((nodes,) + halves, jnp.bfloat16),
            dma((5,)), dma((4,)), dma((12,)),
        ],
        compiler_params=pltpu.CompilerParams(collective_id=0, has_side_effects=True),
        name="layer",
    )(features, weight, degree[None, :], tile_cols, tile_count[None, :], tile_codes, cotangent)
    return pl.pallas_call(
        write_out_kernel,
        out_shape=tuple(jax.ShapeDtypeStruct(shape, dtype) for shape, dtype in outs),
        in_specs=[vmem] * 3,
        out_specs=(pl.BlockSpec(memory_space=pl.ANY),) * 3,
        scratch_shapes=[dma((3,))],
        name="write_out",
    )(*[pltpu.with_memory_space_constraint(x, pltpu.VMEM) for x in results])


def solution(mesh):
    in_specs = (
        P("nodes", "cols"),
        P(None, "cols"),
        P("nodes"),
        P("nodes", None),
        P("nodes"),
        P("nodes", None),
        P("nodes", "cols"),
    )
    out_specs = (P("nodes", "cols"), P(None, "cols"), P("nodes", "cols"))
    local = body
    shape = (mesh.shape["nodes"], mesh.shape["cols"])
    if shape == FUSED_SHAPE:
        local = functools.partial(fused, *shape)
    return jax.shard_map(local, mesh=mesh, in_specs=in_specs, out_specs=out_specs, check_vma=False)
```

```python
import functools

import jax
import jax.numpy as jnp
from jax import lax
from jax.experimental import pallas as pl
from jax.experimental.pallas import tpu as pltpu
from jax.sharding import PartitionSpec as P

MESH = pl.DeviceIdType.MESH

TILE = 128


def tile_bits(pattern_code):
    line_ids = jnp.arange(TILE, dtype=jnp.int32)
    hashed = (
        pattern_code[..., None, None] * 73856093
        ^ line_ids[:, None] * 19349663
        ^ line_ids[None, :] * 83492791
    )
    hashed = hashed ^ hashed >> 13
    hashed = hashed * 1274126177
    hashed = hashed ^ hashed >> 16
    return hashed & 63 == 0


def make_tiles(matches, code_table, live_limit, own, identity):
    slot_ids = jnp.arange(matches.shape[1], dtype=jnp.int32)
    slot_index = jnp.sum(jnp.where(matches, slot_ids[None, :], 0), axis=1, dtype=jnp.int32)
    code_value = jnp.sum(jnp.where(matches, code_table, 0), axis=1, dtype=jnp.int32)
    pattern = tile_bits(code_value) & (slot_index < live_limit)[:, None, None]
    values = (
        pattern.astype(jnp.float32)
        + jnp.where(own, 1.0, 0.0).astype(jnp.float32)[:, None, None] * identity
    )
    return values.astype(jnp.bfloat16)


def body(features, weight, degree, tile_cols, tile_count, tile_codes, cotangent):
    my_block = lax.axis_index("nodes")
    identity = jnp.eye(TILE, dtype=jnp.float32)
    inv_root = lax.rsqrt(degree.astype(jnp.float32))[:, None]
    scaled = (features.astype(jnp.float32) * inv_root).astype(jnp.bfloat16)
    my_cols = tile_cols[0]
    my_codes = tile_codes[0]
    my_count = tile_count[0]
    pieces = lax.all_gather(scaled[None], "nodes", axis=0, tiled=True)
    count_blocks = pieces.shape[0]
    targets = jnp.arange(count_blocks, dtype=jnp.int32)
    matches = targets[:, None] == my_cols[None, :]
    tiles = make_tiles(matches, my_codes[None, :], my_count, targets == my_block, identity)
    gathered = lax.dot_general(
        tiles, pieces, (((0, 2), (0, 1)), ((), ())), preferred_element_type=jnp.float32
    )
    aggregated = (inv_root * gathered).astype(jnp.bfloat16)
    agg_full = lax.all_gather(aggregated, "cols", axis=1, tiled=True)
    pre = jnp.dot(agg_full, weight, preferred_element_type=jnp.float32)
    activation = jax.nn.silu(pre).astype(jnp.bfloat16)
    sigma = jax.nn.sigmoid(pre)
    grad_pre = (cotangent.astype(jnp.float32) * sigma * (1.0 + pre * (1.0 - sigma))).astype(
        jnp.bfloat16
    )
    partial_grad = lax.dot_general(
        agg_full, grad_pre, (((0,), (0,)), ((), ())), preferred_element_type=jnp.float32
    )
    weight_grad = lax.psum(partial_grad, "nodes")
    terms = lax.dot_general(
        grad_pre, weight, (((1,), (1,)), ((), ())), preferred_element_type=jnp.float32
    )
    grad_agg = lax.psum_scatter(terms, "cols", scatter_dimension=1, tiled=True)
    grad_scaled = (inv_root * grad_agg).astype(jnp.bfloat16)
    all_cols, all_counts, all_codes = (
        lax.all_gather(tile_cols, "nodes", axis=0, tiled=True),
        lax.all_gather(tile_count, "nodes", axis=0, tiled=True),
        lax.all_gather(tile_codes, "nodes", axis=0, tiled=True),
    )
    pieces = lax.all_gather(grad_scaled[None], "nodes", axis=0, tiled=True)
    count_blocks = pieces.shape[0]
    row_ids = jnp.arange(count_blocks, dtype=jnp.int32)
    tiles = make_tiles(all_cols == my_block, all_codes, all_counts, row_ids == my_block, identity)
    back_total = lax.dot_general(
        tiles, pieces, (((0, 1), (0, 1)), ((), ())), preferred_element_type=jnp.float32
    )
    feats_grad = inv_root * back_total
    return (activation, weight_grad, feats_grad)


FUSED_SHAPE = (8, 4)

X, META, COT, W, Y, XT, U, WG, GRAD, ACT, Y_NEAR, Y_FAR = range(12)
SENDS = {META: 0, X: 1, COT: 1, W: 1, Y: 1, XT: 2, U: 2, GRAD: 2, WG: 3, ACT: 3}


def dot(a, b, dims):
    return lax.dot_general(a, b, (dims, ((), ())), preferred_element_type=jnp.float32)


def mul(a, b):
    return dot(a, b, ((1,), (0,)))


def turn(block):
    return jnp.transpose(block.astype(jnp.float32)).astype(jnp.bfloat16)


def hash_tile(code, base):
    hashed = (code * 73856093) ^ base
    hashed = hashed ^ hashed >> 13
    hashed = hashed * 1274126177
    hashed = hashed ^ hashed >> 16
    present = jnp.where(code >= 0, 1.0, 0.0)
    return jnp.where(hashed & 63 == 0, present, 0.0).astype(jnp.bfloat16)


def lanes(block):
    return pl.ds(pl.multiple_of(block * TILE, TILE), TILE)


def fused_kernel(
    nodes, cols,
    features_hbm, weight_hbm, degree_hbm, tile_cols_hbm, tile_count_hbm, tile_codes_hbm, cotangent_hbm,
    activation, weight_grad, feats_grad,
    features, weight, degree, tables, tile_count, cotangent,
    x_all, x_in, w_turned, w_all, cot_out, cot_in, meta, base, base_t, eye, adj_t, adj_own,
    y_out, y_in, d_row, agg, pre, grad, act_out, act_all, u_out, u_all, wg_all,
    load_sem, send_sem, recv_sem,
):
    n = lax.axis_index("nodes")
    c = lax.axis_index("cols")
    chips = nodes // 2
    chip, core = n // 2, lax.rem(n, 2)
    x_chip = chip + 1 - 2 * lax.rem(chip, 2)
    y_chip = lax.rem(chip + 2, chips)
    far_chip = lax.rem(x_chip + 2, chips)
    other = 1 - core
    partner = 2 * chip + other
    node_peers = [
        (2 * far_chip + core, core), (2 * far_chip + other, other),
        (2 * x_chip + core, core), (2 * x_chip + other, other),
        (2 * y_chip + core, core), (2 * y_chip + other, other),
        (partner, other),
    ]
    col_peers = [lax.rem(c + d, cols) for d in range(1, cols)]
    half = TILE // 2

    orders = ((3, 2, 1), (2, 3, 0), (3, 0, 1), (0, 1, 2))
    x_order = [sum(jnp.where(c == at, order[i], 0) for at, order in enumerate(orders)) for i in range(cols - 1)]

    barrier = pltpu.get_barrier_semaphore()
    greeted = [(n, peer) for peer in x_order] + [(partner, peer) for peer in x_order]
    greeted += [(peer, c) for peer, _ in node_peers]
    for peer in greeted:
        pl.semaphore_signal(barrier, inc=1, device_id=peer, device_id_type=MESH)

    loads = []
    for i, (src, dst) in enumerate((
        (features_hbm, features), (tile_count_hbm, tile_count), (degree_hbm, degree),
        (tile_cols_hbm, tables.at[pl.ds(0, 1)]), (tile_codes_hbm, tables.at[pl.ds(1, 1)]),
        (cotangent_hbm, cotangent), (weight_hbm, weight),
    )):
        loads.append(pltpu.make_async_copy(src, dst, load_sem.at[(0, 1, 2, 3, 3, 4, 4)[i]]))
        loads[-1].start()

    def push(src, dst, peer, send, recv=None):
        pltpu.make_async_remote_copy(
            src_ref=src, dst_ref=dst, send_sem=send_sem.at[SENDS[send]], recv_sem=recv_sem.at[send if recv is None else recv],
            device_id=peer, device_id_type=MESH,
        ).start()

    def push_nodes(src_of, dst, send, far, near):
        recv = [far, far, send, send, send, send, near]
        for i, (peer, side) in enumerate(node_peers):
            push(src_of(peer, side), dst, (peer, c), send, recv[i])

    def wait_for(like, count, sem):
        whole = like if count == 0 else like.at[pl.ds(0, count)]
        pltpu.make_async_copy(whole, whole, sem).wait()

    def landed(like, count, recv):
        wait_for(like, count, recv_sem.at[recv])

    def left(tiles, send):
        wait_for(adj_t.at[0], tiles * (half * TILE // adj_t.shape[2]), send_sem.at[SENDS[send]])

    loads[0].wait()
    x_all[pl.ds(2 * c, 2)] = turn(features[...]).reshape(2, half, TILE)

    pl.semaphore_wait(barrier, len(greeted))

    for peer in x_order:
        push(x_all.at[pl.ds(2 * c, 2)], x_all.at[pl.ds(2 * c, 2)], (n, peer), X)

    for load in loads[1:3]:
        load.wait()
    wait_for(tables, 0, load_sem.at[3])
    for block in range(nodes):
        code = jnp.int32(-1)
        for slot in range(nodes):
            hit = (tables[0, slot] == block) & (slot < tile_count[0, 0])
            code = jnp.where(hit, tables[1, slot], code)
        meta[n, block] = jnp.full((1, TILE), code, jnp.int32)
    meta[n, nodes] = degree[...]
    push_nodes(lambda peer, side: meta.at[n], meta.at[n], META, META, META)
    wait_for(adj_t.at[0], 10 * (half * TILE // adj_t.shape[2]), load_sem.at[4])
    cot_out[...] = turn(cotangent[...]).reshape(2, half, TILE)
    push_nodes(lambda peer, side: cot_out.at[side], cot_in.at[n], COT, COT, COT)
    cot_in[n] = cot_out[core]

    row_ids = lax.broadcasted_iota(jnp.int32, (TILE, TILE), 0)
    lane_ids = lax.broadcasted_iota(jnp.int32, (TILE, TILE), 1)
    eye[...] = jnp.where(row_ids == lane_ids, 1.0, 0.0).astype(jnp.bfloat16)
    base[...] = row_ids * 19349663 ^ lane_ids * 83492791
    base_t[...] = lane_ids * 19349663 ^ row_ids * 83492791
    for q in range(cols):
        w_turned[:, q * TILE:(q + 1) * TILE] = turn(weight[q * TILE:(q + 1) * TILE, :])
    w_all[c] = weight[lanes(c), :]

    def inv_row(row):
        return lax.rsqrt(meta[row, nodes].astype(jnp.float32))

    def make_row(row):
        d_row[:, lanes(row)] = inv_row(row)
        for block in range(nodes):
            at = (block % 2) * TILE
            adj_t[block // 2, at:at + TILE, lanes(row)] = hash_tile(meta[row, block], base_t[...])
        for side in range(2):
            at = side * TILE
            adj_own[lanes(row), at:at + TILE] = hash_tile(meta[row, 2 * chip + side], base[...])
        own = (row // 2, lanes(lax.rem(row, 2)), lanes(row))
        adj_t[own] = adj_t[own] + eye[...]

    make_row(n)
    landed(x_all, 2 * (cols - 1), X)
    y = mul(w_turned[...], x_all[...].reshape(cols * TILE, TILE)) * inv_row(n)
    y_out[...] = y.astype(jnp.bfloat16).reshape(2, half, TILE)
    push_nodes(lambda peer, side: y_out.at[side], y_in.at[n], Y, Y_FAR, Y_NEAR)
    push_nodes(lambda peer, side: x_all.at[peer], x_in.at[n], XT, XT, XT)
    for peer in col_peers:
        push(weight.at[lanes(peer), :], w_all.at[c], (n, peer), W)
    y_in[n] = y_out[core]
    x_in[n] = x_all[n]

    landed(meta, nodes - 1, META)
    make_row(partner)
    for side in range(2):
        own = (lanes(2 * chip + side), slice(side * TILE, (side + 1) * TILE))
        adj_own[own] = adj_own[own] + eye[...]

    def make_far(i, carry):
        make_row(lax.rem(2 * chip + i, nodes))
        return carry

    lax.fori_loop(2, nodes, make_far, 0)

    def chip_pair(buffer, at):
        return jnp.concatenate([buffer[2 * at], buffer[2 * at + 1]], axis=1)

    landed(cot_in, nodes - 1, COT)
    landed(y_in, 1, Y_NEAR)
    pre[...] = mul(chip_pair(y_in, chip), adj_t[chip])
    landed(y_in, 4, Y)
    pre[...] += mul(chip_pair(y_in, x_chip), adj_t[x_chip]) + mul(chip_pair(y_in, y_chip), adj_t[y_chip])
    landed(y_in, 2, Y_FAR)
    inv = d_row[...]
    value = (pre[...] + mul(chip_pair(y_in, far_chip), adj_t[far_chip])) * inv
    pre[...] = value
    sigma = 0.5 * jnp.tanh(0.5 * value) + 0.5
    cot = jnp.concatenate([cot_in[block] for block in range(nodes)], axis=1).astype(jnp.float32)
    grad[core] = (inv * (cot * sigma * (1.0 + value * (1.0 - sigma)))).astype(jnp.bfloat16)
    u = mul(grad[core], adj_own[...])
    for side in range(2):
        u_out[side] = (u[:, side * TILE:(side + 1) * TILE] * inv_row(2 * chip + side)).astype(jnp.bfloat16)
    here = u_all.at[2 * c + core]
    for peer in col_peers:
        push(u_out.at[core], here, (n, peer), U)
        push(u_out.at[other], here, (partner, peer), U)
    push(u_out.at[other], here, (partner, c), U)
    u_all[2 * c + core] = u_out[core]

    push(grad.at[core], grad.at[core], (partner, c), GRAD)
    for side, block in enumerate((n, partner)):
        own = pre[:, lanes(block)]
        act_out[side] = (own * jax.nn.sigmoid(own)).astype(jnp.bfloat16)
    push(act_out.at[1], act_all.at[core], (partner, c), ACT)
    act_all[core] = act_out[0]

    landed(x_in, nodes - 1, XT)
    scaled = jnp.concatenate([
        (x_in[block].astype(jnp.float32) * inv_row(block)).astype(jnp.bfloat16) for block in range(nodes)
    ], axis=1)
    for i in range(chips):
        part = slice(2 * i * TILE, 2 * (i + 1) * TILE)
        agg[:, part] = mul(scaled, adj_t[:, :, part].reshape(nodes * TILE, 2 * TILE)).astype(jnp.bfloat16)
    landed(grad, 1, GRAD)
    wg_all[n] = dot(agg[...], grad[...].reshape(TILE, nodes * TILE), ((1,), (1,))).astype(wg_all.dtype)
    push_nodes(lambda peer, side: wg_all.at[n], wg_all.at[n], WG, WG, WG)
    landed(act_all, 1, ACT)
    activation[...] = turn(act_all[...].reshape(TILE, TILE))

    wait_for(meta, nodes - 1, send_sem.at[SENDS[META]])
    left(4 * (cols - 1) + 2 * (nodes - 1), Y)
    left(nodes - 1 + 2 * cols - 1 + nodes, U)
    landed(w_all, cols - 1, W)
    landed(u_all, 2 * cols - 1, U)
    w_wide = jnp.concatenate([w_all[q] for q in range(cols)], axis=1)
    feats_grad[...] = jnp.transpose(mul(w_wide, u_all[...].reshape(cols * TILE, TILE)))

    landed(wg_all, nodes - 1, WG)
    for block in range(nodes):
        weight_grad[block * half:(block + 1) * half, :] = wg_all[block].astype(jnp.float32)
    left(nodes, WG)


def write_out_kernel(*refs):
    count = len(refs) // 2
    copies = [pltpu.make_async_copy(refs[i], refs[count + i], refs[-1].at[i]) for i in range(count)]
    for copy in copies:
        copy.start()
    for copy in copies:
        copy.wait()


def fused(nodes, cols, features, weight, degree, tile_cols, tile_count, tile_codes, cotangent):
    hbm = pl.BlockSpec(memory_space=pltpu.HBM)
    vmem = pl.BlockSpec(memory_space=pltpu.VMEM)
    block = (TILE, TILE)
    halves = (TILE // 2, TILE)
    total = nodes * TILE
    outs = ((features.shape, jnp.bfloat16), (weight.shape, jnp.float32), (features.shape, jnp.float32))
    dma = pltpu.SemaphoreType.DMA
    results = pl.pallas_call(
        functools.partial(fused_kernel, nodes, cols),
        out_shape=tuple(pltpu.VMEM(shape, dtype) for shape, dtype in outs),
        in_specs=[hbm] * 7,
        out_specs=(vmem, vmem, vmem),
        scratch_shapes=[
            pltpu.VMEM(features.shape, jnp.bfloat16),
            pltpu.VMEM(weight.shape, jnp.bfloat16),
            pltpu.VMEM((1, TILE), jnp.int32),
            pltpu.SMEM((2,) + tile_cols.shape[1:], jnp.int32),
            pltpu.SMEM((1, 1), jnp.int32),
            pltpu.VMEM(cotangent.shape, jnp.bfloat16),
            pltpu.VMEM((2 * cols,) + halves, jnp.bfloat16),
            pltpu.VMEM((nodes,) + halves, jnp.bfloat16),
            pltpu.VMEM((TILE, weight.shape[0]), jnp.bfloat16),
            pltpu.VMEM((cols,) + block, jnp.bfloat16),
            pltpu.VMEM((2,) + halves, jnp.bfloat16),
            pltpu.VMEM((nodes,) + halves, jnp.bfloat16),
            pltpu.VMEM((nodes, nodes + 1, 1, TILE), jnp.int32),
            pltpu.VMEM(block, jnp.int32),
            pltpu.VMEM(block, jnp.int32),
            pltpu.VMEM(block, jnp.bfloat16),
            pltpu.VMEM((nodes // 2, 2 * TILE, total), jnp.bfloat16),
            pltpu.VMEM((total, 2 * TILE), jnp.bfloat16),
            pltpu.VMEM((2,) + halves, jnp.bfloat16),
            pltpu.VMEM((nodes,) + halves, jnp.bfloat16),
            pltpu.VMEM((1, total), jnp.float32),
            pltpu.VMEM((TILE // 2, total), jnp.bfloat16),
            pltpu.VMEM((TILE // 2, total), jnp.float32),
            pltpu.VMEM((2, TILE // 2, total), jnp.bfloat16),
            pltpu.VMEM((2,) + halves, jnp.bfloat16),
            pltpu.VMEM((2,) + halves, jnp.bfloat16),
            pltpu.VMEM((2,) + halves, jnp.bfloat16),
            pltpu.VMEM((2 * cols,) + halves, jnp.bfloat16),
            pltpu.VMEM((nodes,) + halves, jnp.bfloat16),
            dma((5,)), dma((4,)), dma((12,)),
        ],
        compiler_params=pltpu.CompilerParams(collective_id=0, has_side_effects=True),
        name="layer",
    )(features, weight, degree[None, :], tile_cols, tile_count[None, :], tile_codes, cotangent)
    return pl.pallas_call(
        write_out_kernel,
        out_shape=tuple(jax.ShapeDtypeStruct(shape, dtype) for shape, dtype in outs),
        in_specs=[vmem] * 3,
        out_specs=(pl.BlockSpec(memory_space=pl.ANY),) * 3,
        scratch_shapes=[dma((3,))],
        name="write_out",
    )(*[pltpu.with_memory_space_constraint(x, pltpu.VMEM) for x in results])


def solution(mesh):
    in_specs = (
        P("nodes", "cols"),
        P(None, "cols"),
        P("nodes"),
        P("nodes", None),
        P("nodes"),
        P("nodes", None),
        P("nodes", "cols"),
    )
    out_specs = (P("nodes", "cols"), P(None, "cols"), P("nodes", "cols"))
    local = body
    shape = (mesh.shape["nodes"], mesh.shape["cols"])
    if shape == FUSED_SHAPE:
        local = functools.partial(fused, *shape)
    return jax.shard_map(local, mesh=mesh, in_specs=in_specs, out_specs=out_specs, check_vma=False)
```
